256 devices in a mesh: member: 16 (over y, x_hi, core), dp: 16 (over z, x_lo).
Axes of the slice: x: 4 (x_hi: 2, x_lo: 2; x = x_hi * 2 + x_lo), y: 4, z: 8, core: 2. Of those that a mesh axis runs over, the one named last changes fastest.
Arguments:
- teacher_tokens: bfloat16 [2752, 1536], P('dp'), may hold values from -100 to 100
- teacher_qkv: bfloat16 [16, 1536, 4608], P('member', None, 'dp'), may hold values from -0.15625 to 0.15625
- student_tokens: bfloat16 [2752, 1024], P('dp'), may hold values from -6 to 6
- student_gain: float32 [1024], replicated, may hold values from 0.1 to 1.9
- w_up: bfloat16 [1024, 4096], P(None, 'member'), may hold values from -0.1875 to 0.1875
- w_down: bfloat16 [1024, 4096], P(None, 'member'), may hold values from -0.09375 to 0.09375
- w_head: bfloat16 [1024, 1536], P(None, 'member'), may hold values from -0.1875 to 0.1875
Outputs:
- grad_up: float32 [1024, 4096], P('dp', 'member')
- grad_down: float32 [1024, 4096], P('dp', 'member')
- grad_head: float32 [1024, 1536], P('dp', 'member')
The draws below stay inside these ranges and needn't reach their ends.
All inputs are finite; a program needn't handle non-finite values.
Results may differ from the reference program's by a relative error of at most 0.0055.
Values may be sent and summed in bfloat16 or wider, within the bound.
No kernel may reach another device: no remote copies, remote signals or barrier semaphores. Data moves between devices by JAX's collectives and lax.ppermute only.
A program may use at most 192 MiB of HBM per device.

```python
import math
from functools import partial
import jax
import jax.numpy as jnp
from jax import lax

DT = 1536
HEAD = 64
DS = 1024
FF = 4096
VALID = 1370
IMAGES = 2
TOKENS = 2752
MEMBERS = 16


def draw_teacher_tokens(key, part):
    key_base = jax.random.fold_in(key, 0)
    values = 1.6 * jnp.clip(jax.random.normal(key_base, (TOKENS, DT), jnp.float32), -6.0, 6.0)
    return values.astype(jnp.bfloat16)


def level_of(own_key, shape, cuts, low, largest):
    gain = 1.0
    for axis_at, blocks in cuts:
        heights = jax.random.uniform(jax.random.fold_in(jax.random.fold_in(own_key, 6), axis_at), (blocks,), jnp.float32, low / len(cuts), largest / len(cuts))
        gain = gain * jnp.repeat(jnp.exp(heights), shape[axis_at] // blocks).reshape((-1,) + (1,) * (len(shape) - 1 - axis_at))
    return gain


def scatter_about(key, shape, width, reach, cuts=(), kind=jnp.bfloat16):
    level = level_of(key, shape, cuts, -0.22, 0.18) if cuts else 1.0
    drawn = jax.random.normal(key, shape, jnp.float32) * width * level
    return jnp.minimum(jnp.maximum(drawn, -reach), reach).astype(kind)


def setup_inputs(seed: int = 0) -> dict:
    arg_keys = jax.random.split(jax.random.key(seed), 8)
    teacher_tokens = draw_teacher_tokens(jax.random.fold_in(arg_keys[7], 71), 0)
    teacher_qkv = scatter_about(arg_keys[1], (MEMBERS, DT, 3 * DT), DT ** -0.5, 0.15625, ((0, 16), (2, 16)))
    student_tokens = scatter_about(arg_keys[2], (TOKENS, DS), 1.0, 6.0, ((0, 16),))
    student_gain = jnp.clip(1.0 + 0.18 * jax.random.normal(arg_keys[3], (DS,), jnp.float32), 0.1, 1.9)
    w_up = scatter_about(arg_keys[4], (DS, FF), DS ** -0.5, 0.1875, ((1, 16),))
    w_down = scatter_about(arg_keys[5], (DS, FF), FF ** -0.5, 0.09375, ((1, 16),))
    w_head = scatter_about(arg_keys[6], (DS, DT), DS ** -0.5, 0.1875, ((1, 16),))
    return dict(teacher_tokens=teacher_tokens, teacher_qkv=teacher_qkv, student_tokens=student_tokens, student_gain=student_gain, w_up=w_up, w_down=w_down, w_head=w_head)


def reference(teacher_tokens, teacher_qkv, student_tokens, student_gain, w_up, w_down, w_head):
    head_count = DT // HEAD
    slots = jnp.arange(TOKENS, dtype=jnp.int32)
    image_of = slots % IMAGES
    real_slot = slots // IMAGES < VALID
    allowed = (image_of[:, None] == image_of[None, :]) & real_slot[None, :]

    def split_heads(block):
        return block.reshape(TOKENS, head_count, HEAD).transpose(1, 0, 2)

    def one_head(operands):
        query_head, key_head, value_head = operands
        scores = jnp.dot(query_head, key_head.T, preferred_element_type=jnp.float32) * 0.125
        scores = jnp.where(allowed, scores, -1e+30)
        top_score = lax.optimization_barrier(jnp.max(scores, axis=-1, keepdims=True))
        expsc = jnp.where(allowed, jnp.exp(scores - top_score), 0.0)
        denom_sum = lax.optimization_barrier(jnp.sum(expsc, axis=-1, keepdims=True))
        return jnp.dot(expsc.astype(jnp.bfloat16), value_head, preferred_element_type=jnp.float32) / denom_sum

    def member_context(running, weight):
        projected = jnp.dot(teacher_tokens, weight, preferred_element_type=jnp.float32).astype(jnp.bfloat16)
        queries = split_heads(projected[:, :DT])
        keys_all = split_heads(projected[:, DT:2 * DT])
        values_all = split_heads(projected[:, 2 * DT:])
        context = lax.map(one_head, (queries, keys_all, values_all))
        return (running + context.transpose(1, 0, 2).reshape(TOKENS, DT), None)
    summed, _ = lax.scan(member_context, jnp.zeros((TOKENS, DT), jnp.float32), teacher_qkv)
    row_mean = lax.optimization_barrier(jnp.mean(summed, axis=-1, keepdims=True))
    mean_square = lax.optimization_barrier(jnp.mean(summed * summed, axis=-1, keepdims=True))
    target = (summed - row_mean) * lax.rsqrt(mean_square - row_mean * row_mean + 1e-06)
    inputs = student_tokens.astype(jnp.float32)
    in_mean = lax.optimization_barrier(jnp.mean(inputs, axis=-1, keepdims=True))
    in_var = lax.optimization_barrier(jnp.mean((inputs - in_mean) ** 2, axis=-1, keepdims=True))
    normed = ((inputs - in_mean) * lax.rsqrt(in_var + 1e-06) * student_gain).astype(jnp.bfloat16)
    pre = jnp.dot(normed, w_up, preferred_element_type=jnp.float32)
    gelu_tanh = partial(jax.nn.gelu, approximate=True)
    hidden = gelu_tanh(pre).astype(jnp.bfloat16)
    branch = lax.dot_general(hidden, w_down, (((1,), (1,)), ((), ())), preferred_element_type=jnp.float32)
    student_out = (inputs + branch).astype(jnp.bfloat16)
    pred = jnp.dot(student_out, w_head, preferred_element_type=jnp.float32)
    pred_grad = jnp.where(real_slot[:, None], (pred - target) / math.sqrt(IMAGES * VALID), 0.0).astype(jnp.bfloat16)
    grad_head = lax.dot_general(student_out, pred_grad, (((0,), (0,)), ((), ())), preferred_element_type=jnp.float32)
    out_grad = lax.dot_general(pred_grad, w_head, (((1,), (1,)), ((), ())), preferred_element_type=jnp.float32).astype(jnp.bfloat16)
    grad_down = lax.dot_general(out_grad, hidden, (((0,), (0,)), ((), ())), preferred_element_type=jnp.float32)
    hidden_grad = jnp.dot(out_grad, w_down, preferred_element_type=jnp.float32)
    _, pullback = jax.vjp(gelu_tanh, pre)
    pre_grad = pullback(hidden_grad)[0].astype(jnp.bfloat16)
    grad_up = lax.dot_general(normed, pre_grad, (((0,), (0,)), ((), ())), preferred_element_type=jnp.float32)
    return (grad_up, grad_down, grad_head)
```

```python
from functools import partial
import math

import jax
import jax.numpy as jnp
from jax import lax
from jax.experimental import pallas as pl
from jax.experimental.pallas import tpu as pltpu
from jax.sharding import Mesh, PartitionSpec as P

VALID = 1370
IMAGES = 2
BF = jnp.bfloat16
F32 = jnp.float32
MEM = ("y", "xh", "c")
G = ("y", "xh")
DP = ("z", "xl")
GROUP = (0, 2, 1, 3, 5, 7, 4, 6)
AT = tuple(GROUP.index(j) for j in range(8))
SWAP = [(0, 1), (1, 0)]
CHUNK = 86
ROWS = 88


def teacher_kernel(s_ref, xa0, xa1, xa2, xa3, xb0, xb1, xb2, xb3, m_own, m_oth, h_own, h_oth, out_ref, xs, wt, p_sc, vx):
    y, xl, rot, c, z = s_ref[0], s_ref[1], s_ref[2], s_ref[3], s_ref[4]
    half = 8 * ROWS
    total = 2 * half
    for d, (a, b) in enumerate(((xa0, xb0), (xa1, xb1), (xa2, xb2), (xa3, xb3))):
        col = pl.multiple_of(lax.rem(y + d, 4) * 384, 384)
        xs[0:half, pl.ds(col, 384)] = a[...]
        xs[half:total, pl.ds(col, 384)] = b[...]
    wt[pl.ds(pl.multiple_of(xl * 384, 384), 192), :] = m_own[...]
    wt[pl.ds(pl.multiple_of((1 - xl) * 384, 384), 192), :] = m_oth[...]
    wt[pl.ds(pl.multiple_of(192 + xl * 96, 96), 96), :] = h_own[...]
    wt[pl.ds(pl.multiple_of(192 + (1 - xl) * 96, 96), 96), :] = h_oth[...]
    blk = 176

    def project(i, carry):
        r0 = pl.multiple_of(i * blk, blk)
        out = lax.dot_general(xs[pl.ds(r0, blk), :], wt[...], (((1,), (1,)), ((), ())), preferred_element_type=F32).astype(BF)
        for t in range(9):
            p_sc[t, pl.ds(r0, blk), :] = out[:, 64 * t : 64 * t + 64]
        return carry

    lax.fori_loop(0, total // blk, project, 0)
    q0 = 3 * rot
    k0 = 3 * lax.rem(rot + 2, 3)
    v0 = 3 * lax.rem(rot + 1, 3)
    row = lax.broadcasted_iota(jnp.int32, (total, 1), 0)
    second = row >= half
    r = lax.rem(row, ROWS)
    zz = lax.rem(row // ROWS, 8)
    parity = jnp.where(second, 1 - c, c)
    real = r < jnp.where((zz == 7) & (parity == 1), VALID - 15 * CHUNK, CHUNK)
    realf = real.astype(F32)
    lane = lax.broadcasted_iota(jnp.int32, (total, 64), 1)
    ones = jnp.where(lane == 0, realf, 0.0).astype(BF)
    for h in range(3):
        vals = p_sc[v0 + h].astype(F32) * realf
        vx[h, :, 0:64] = vals.astype(BF)
        vx[h, :, 64:128] = ones

    def attend(i, carry):
        r0 = pl.multiple_of(i * blk, blk)
        for h in range(3):
            q = p_sc[q0 + h, pl.ds(r0, blk), :] * jnp.asarray(0.125, BF)
            s = lax.dot_general(q, p_sc[k0 + h], (((1,), (1,)), ((), ())), preferred_element_type=F32)
            m = jnp.max(s, axis=1, keepdims=True)
            p = jnp.exp(s - m).astype(BF)
            o = jnp.dot(p, vx[h], preferred_element_type=F32)
            out_ref[pl.ds(r0, blk), 64 * h : 64 * h + 64] = o[:, 0:64] / o[:, 64:65]
        return carry

    lax.fori_loop(0, total // blk, attend, 0)


def teacher(scalars, xa, xb, m_own, m_oth, h_own, h_oth):
    total = 16 * ROWS
    vm = pl.BlockSpec(memory_space=pltpu.VMEM)
    return pl.pallas_call(
        teacher_kernel,
        out_shape=jax.ShapeDtypeStruct((total, 192), F32),
        in_specs=[pl.BlockSpec(memory_space=pltpu.SMEM)] + [vm] * 12,
        out_specs=vm,
        scratch_shapes=[
            pltpu.VMEM((total, 1536), BF),
            pltpu.VMEM((576, 1536), BF),
            pltpu.VMEM((9, total, 64), BF),
            pltpu.VMEM((3, total, 128), BF),
        ],
        compiler_params=pltpu.CompilerParams(vmem_limit_bytes=50 * 2**20),
        cost_estimate=pl.CostEstimate(flops=6_000_000_000, bytes_accessed=12_000_000, transcendentals=6_000_000),
        name="teacher",
    )(scalars, *xa, *xb, m_own, m_oth, h_own, h_oth)


def swap(x, axis):
    return lax.ppermute(x, axis, SWAP)


def spread(x, axis, n):
    return lax.all_to_all(jnp.broadcast_to(x[None], (n,) + x.shape), axis, 0, 0, tiled=True)


def body(teacher_tokens, teacher_qkv, student_tokens, student_gain, w_up, w_down, w_head):
    y, xh, c, z, xl = (lax.axis_index(a) for a in ("y", "xh", "c", "z", "xl"))
    g = 2 * y + xh

    wt = teacher_qkv[0].T
    main = jnp.where(xl == 0, wt[:192], wt[96:])
    part = jnp.where(xl == 0, wt[192:], wt[:96])
    to_main = [(2 * k + e, 2 * AT[(3 * k + 2 * e) % 8] + e) for k in range(8) for e in range(2)]
    to_part = [(2 * k + e, 2 * AT[(3 * k + 1) % 8] + e) for k in range(8) for e in range(2)]
    m_own = lax.ppermute(main, DP, to_main)
    h_own = lax.ppermute(part, DP, to_part)
    m_oth = swap(m_own, "xl")
    h_oth = swap(h_own, "xl")

    tt = lax.dynamic_slice_in_dim(teacher_tokens, y * 384, 384, 1).reshape(CHUNK, IMAGES, 384)
    rows = jnp.arange(ROWS)[:, None]
    reals = jnp.where((z == 7) & (xl == 1), VALID - 15 * CHUNK, CHUNK)

    def padded(v):
        v = jnp.pad(v, ((0, ROWS - CHUNK), (0, 0)))
        return jnp.where(rows < reals, v, v[79:80])

    mine = padded(jnp.where(xl == 0, tt[:, 0], tt[:, 1]))
    other = padded(jnp.where(xl == 0, tt[:, 1], tt[:, 0]))
    got = lax.ppermute(other, ("c", "xl"), [(0, 1), (3, 2)])
    piece = jnp.where(c == xl, mine, got)
    xa0 = spread(piece, "z", 8).reshape(8 * ROWS, 384)
    xa1 = lax.ppermute(xa0, "y", [(k, (k - 1) % 4) for k in range(4)])
    xa3 = lax.ppermute(xa0, "y", [(k, (k + 1) % 4) for k in range(4)])
    top = lax.ppermute(xa1[: 4 * ROWS], "y", [(k, (k - 1) % 4) for k in range(4)])
    low = lax.ppermute(xa3[4 * ROWS :], "y", [(k, (k + 1) % 4) for k in range(4)])
    xa2 = jnp.concatenate([top, low])
    xa = (xa0, xa1, xa2, xa3)
    xb = tuple(swap(v, "c") for v in xa)

    def arranged(v):
        v = jnp.pad(v, ((0, (ROWS - CHUNK) * IMAGES), (0, 0))).reshape(11, 8, IMAGES, -1)
        return v.transpose(2, 1, 0, 3).reshape(IMAGES, ROWS, -1)

    st_own = arranged(student_tokens)
    st_nb = swap(jnp.where(c == 0, st_own[0], st_own[1]), "xl")
    st_nb2 = swap(st_nb, "c")
    st_oth = jnp.where(c == 0, jnp.stack([st_nb, st_nb2]), jnp.stack([st_nb2, st_nb]))
    st = jnp.where(xl == 0, jnp.stack([st_own, st_oth]), jnp.stack([st_oth, st_own]))
    inputs = st.reshape(4 * ROWS, -1).astype(F32)
    in_mean = jnp.mean(inputs, axis=-1, keepdims=True)
    in_var = jnp.mean((inputs - in_mean) ** 2, axis=-1, keepdims=True)
    normed = ((inputs - in_mean) * lax.rsqrt(in_var + 1e-06) * student_gain).astype(BF)
    up = lax.dynamic_slice_in_dim(w_up, xl * 128, 128, 1)
    down = lax.dynamic_slice_in_dim(w_down, xl * 128, 128, 1)
    pre = jnp.dot(normed, up, preferred_element_type=F32)
    gelu_tanh = partial(jax.nn.gelu, approximate=True)
    hidden = gelu_tanh(pre).astype(BF)
    branch = lax.dot_general(hidden, down, (((1,), (1,)), ((), ())), preferred_element_type=F32)
    branch = branch.reshape(2, 2, ROWS, -1)
    keep = lax.dynamic_index_in_dim(branch, c, 0, False) + swap(lax.dynamic_index_in_dim(branch, 1 - c, 0, False), "c")
    sent = swap(lax.dynamic_index_in_dim(keep, 1 - xl, 0, False).astype(BF), "xl")
    keep = (lax.dynamic_index_in_dim(keep, xl, 0, False) + sent.astype(F32)).astype(BF)
    keep = lax.all_to_all(keep.reshape(8, 11, -1), G, 0, 0, tiled=True)
    own_in = lax.dynamic_slice(st.reshape(2, 2, 8, 11, -1), (c, xl, g, 0, 0), (1, 1, 1, 11, st.shape[-1]))[0, 0, 0]
    student_out = (own_in.astype(F32) + jnp.sum(keep.astype(F32), axis=0)).astype(BF)

    def regroup(v):
        nb = swap(v, "xl")
        pair = jnp.where(xl == 0, jnp.stack([v, nb]), jnp.stack([nb, v]))
        far = swap(pair, "c")
        return jnp.where(c == 0, jnp.stack([pair, far]), jnp.stack([far, pair]))

    so_all = regroup(spread(student_out, G, 8).reshape(ROWS, -1)).reshape(4 * ROWS, -1)

    wh = w_head.T
    wh, anchor = lax.optimization_barrier((wh, xa2))
    wh2 = swap(wh, "xh")
    pair = jnp.where(xh == 0, jnp.stack([wh, wh2]), jnp.stack([wh2, wh]))
    w_y = [
        pair,
        lax.ppermute(pair, "y", [(k, (k - 1) % 4) for k in range(4)]),
        lax.ppermute(pair, "y", [(k, (k + 2) % 4) for k in range(4)]),
        lax.ppermute(pair, "y", [(k, (k + 1) % 4) for k in range(4)]),
    ]
    w_y = jnp.stack(w_y)
    w_far = swap(w_y, "c")
    w_all = jnp.where(c == 0, jnp.stack([w_y, w_far], axis=2), jnp.stack([w_far, w_y], axis=2))
    w_all = jnp.concatenate([lax.dynamic_index_in_dim(w_all, (k - y) % 4, 0, True) for k in range(4)])
    w_all = w_all.reshape(1536, -1)
    pred = lax.dot_general(student_out, w_all, (((1,), (1,)), ((), ())), preferred_element_type=F32)

    group = jnp.take(jnp.asarray(GROUP, jnp.int32), z)
    scalars = jnp.stack([y, xl, group % 3, c, z]).astype(jnp.int32)
    xa = (xa[0], xa[1], anchor, xa[3])
    context = teacher(scalars, xa, xb, m_own, m_oth, h_own, h_oth)
    context = context.reshape(2, 8 * ROWS, 192)
    both = context[0] + swap(context[1], "c")
    both = both.astype(BF).reshape(8, 11, 8, 192).transpose(2, 0, 1, 3)
    got = lax.all_to_all(both, G, 0, 0, tiled=True)
    sums = jnp.sum(got.astype(F32), axis=0)
    sums = lax.all_to_all(sums, "z", 0, 0, tiled=True)
    summed = jnp.concatenate([sums[AT[j]] for j in range(8)], axis=-1)

    row_mean = jnp.mean(summed, axis=-1, keepdims=True)
    mean_square = jnp.mean(summed * summed, axis=-1, keepdims=True)
    target = (summed - row_mean) * lax.rsqrt(mean_square - row_mean * row_mean + 1e-06)
    r = 8 * jnp.arange(11)[:, None] + g
    real = (r < CHUNK) & (172 * z + CHUNK * c + r < VALID)
    pred_grad = jnp.where(real, (pred - target) / math.sqrt(IMAGES * VALID), 0.0).astype(BF)
    out_grad = jnp.dot(pred_grad, w_all, preferred_element_type=F32).astype(BF)

    cols = pred_grad.reshape(11, 8, 192).transpose(1, 0, 2)
    load = jnp.concatenate([jnp.broadcast_to(out_grad[None], (8,) + out_grad.shape), cols], axis=-1)
    load = lax.all_to_all(load, G, 0, 0, tiled=True).reshape(ROWS, -1)
    load = regroup(load).reshape(4 * ROWS, -1)
    og = load[:, :1024]
    pg = load[:, 1024:]
    pg = jnp.where(c == 0, pg[:, :96], pg[:, 96:])
    pg = jnp.where(xl == 0, pg[:, :48], pg[:, 48:])

    dims = (((0,), (0,)), ((), ()))
    grad_head = lax.dot_general(pg, so_all, dims, preferred_element_type=F32)
    grad_down = lax.dot_general(hidden, og, dims, preferred_element_type=F32)
    hidden_grad = jnp.dot(og, down, preferred_element_type=F32)
    _, pullback = jax.vjp(gelu_tanh, pre)
    pre_grad = pullback(hidden_grad)[0].astype(BF)
    grad_up = lax.dot_general(pre_grad, normed, dims, preferred_element_type=F32)
    grads = jnp.concatenate([grad_up, grad_down, grad_head]).astype(BF)
    grads = grads.reshape(-1, 8, 128).transpose(1, 0, 2)
    grads = lax.all_to_all(grads, "z", 0, 0, tiled=True)
    grads = jnp.sum(grads.astype(F32), axis=0)
    stay = jnp.where(xl == 0, grads[:, :64], grads[:, 64:])
    come = swap(jnp.where(xl == 0, grads[:, 64:], grads[:, :64]), "xl")

    def joined(lo, hi):
        a, b = stay[lo:hi], come[lo:hi]
        return jnp.where(xl == 0, jnp.concatenate([a, b]), jnp.concatenate([b, a])).T

    return joined(0, 128), joined(128, 256), joined(256, 304)


def solution(mesh):
    fine = Mesh(mesh.devices.reshape(4, 2, 2, 8, 2), ("y", "xh", "c", "z", "xl"))
    in_specs = (
        P(DP, None),
        P(MEM, None, DP),
        P(DP, None),
        P(),
        P(None, MEM),
        P(None, MEM),
        P(None, MEM),
    )
    out_specs = (P(DP, MEM), P(DP, MEM), P(DP, MEM))
    return jax.shard_map(body, mesh=fine, in_specs=in_specs, out_specs=out_specs, check_vma=False)
```

```python
import math

import jax
import jax.numpy as jnp
from jax import lax
from jax.experimental import pallas as pl
from jax.experimental.pallas import tpu as pltpu
from jax.sharding import Mesh, PartitionSpec as P

VALID = 1370
IMAGES = 2
BF = jnp.bfloat16
F32 = jnp.float32
MEM = ("y", "xh", "c")
G = ("y", "xh")
DP = ("z", "xl")
GROUP = (0, 2, 1, 3, 5, 7, 4, 6)
AT = tuple(GROUP.index(j) for j in range(8))
SWAP = [(0, 1), (1, 0)]
CHUNK = 86
ROWS = 88


def teacher_kernel(s_ref, xa0, xa1, xa2, xa2l, xa3, xb0, xb1, xb2, xb2l, xb3, m_own, m_oth, h_own, h_oth, own_ref, oth_ref, xs, wt, p_sc, vx):
    y, xl, rot, c = s_ref[0], s_ref[1], s_ref[2], s_ref[3]
    half = 8 * ROWS
    total = 2 * half
    for d, (a, b) in enumerate(((xa0, xb0), (xa1, xb1), ((xa2, xa2l), (xb2, xb2l)), (xa3, xb3))):
        col = pl.multiple_of(lax.rem(y + d, 4) * 384, 384)
        if d == 2:
            for k, v in enumerate((*a, *b)):
                xs[k * half // 2 : (k + 1) * half // 2, pl.ds(col, 384)] = v[...]
        else:
            xs[0:half, pl.ds(col, 384)] = a[...]
            xs[half:total, pl.ds(col, 384)] = b[...]
    wt[pl.ds(pl.multiple_of(xl * 384, 384), 192), :] = m_own[...]
    wt[pl.ds(pl.multiple_of((1 - xl) * 384, 384), 192), :] = m_oth[...]
    wt[pl.ds(pl.multiple_of(192 + xl * 96, 96), 96), :] = h_own[...]
    wt[pl.ds(pl.multiple_of(192 + (1 - xl) * 96, 96), 96), :] = h_oth[...]
    blk = 176

    def project(i, carry):
        r0 = pl.multiple_of(i * blk, blk)
        out = lax.dot_general(xs[pl.ds(r0, blk), :], wt[...], (((1,), (1,)), ((), ())), preferred_element_type=F32).astype(BF)
        for t in range(9):
            p_sc[t, pl.ds(r0, blk), :] = out[:, 64 * t : 64 * t + 64]
        return carry

    lax.fori_loop(0, total // blk, project, 0)
    q0 = 3 * rot
    k0 = 3 * lax.rem(rot + 2, 3)
    v0 = 3 * lax.rem(rot + 1, 3)
    row = lax.broadcasted_iota(jnp.int32, (total, 1), 0)
    second = row >= half
    r = lax.rem(row, ROWS)
    zz = lax.rem(row // ROWS, 8)
    parity = jnp.where(second, 1 - c, c)
    real = r < jnp.where((zz == 7) & (parity == 1), VALID - 15 * CHUNK, CHUNK)
    realf = real.astype(F32)
    lane = lax.broadcasted_iota(jnp.int32, (total, 64), 1)
    ones = jnp.where(lane == 0, realf, 0.0).astype(BF)
    for h in range(3):
        vals = p_sc[v0 + h].astype(F32) * realf
        vx[h, :, 0:64] = vals.astype(BF)
        vx[h, :, 64:128] = ones

    def attend(i, out_ref, base, at):
        r0 = pl.multiple_of(i * blk, blk)
        for h in range(3):
            q = p_sc[q0 + h, pl.ds(base + r0, blk), :] * jnp.asarray(0.125, BF)
            s = lax.dot_general(q, p_sc[k0 + h], (((1,), (1,)), ((), ())), preferred_element_type=F32)
            m = jnp.max(s, axis=1, keepdims=True)
            p = jnp.exp(s - m).astype(BF)
            o = jnp.dot(p, vx[h], preferred_element_type=F32)
            out_ref[pl.ds(r0, blk), at + 64 * h : at + 64 * h + 64] = o[:, 0:64] / o[:, 64:65]

    quarter = half // 2
    for k, (out_ref, at) in enumerate(((oth_ref, 0), (oth_ref, 192), (own_ref, 0), (own_ref, 192))):
        base = (half if k < 2 else 0) + (k % 2) * quarter

        @pl.loop(0, quarter // blk)
        def _(i, out_ref=out_ref, base=base, at=at):
            attend(i, out_ref, base, at)


VM = pl.BlockSpec(memory_space=pltpu.VMEM)
SM = pl.BlockSpec(memory_space=pltpu.SMEM)
TN = (((0,), (0,)), ((), ()))
NT = (((1,), (1,)), ((), ()))


def call(kernel, outs, *args, scratch=(), scalar=0, flops=0, vmem=24):
    shapes = [jax.ShapeDtypeStruct(s, d) for s, d in outs]
    moved = sum(math.prod(v.shape) * v.dtype.itemsize for v in args) + sum(math.prod(s.shape) * s.dtype.itemsize for s in shapes)
    return pl.pallas_call(
        kernel,
        out_shape=shapes,
        in_specs=[SM] * scalar + [VM] * (len(args) - scalar),
        out_specs=[VM] * len(shapes),
        scratch_shapes=list(scratch),
        compiler_params=pltpu.CompilerParams(vmem_limit_bytes=vmem * 2**20),
        cost_estimate=pl.CostEstimate(flops=flops, bytes_accessed=moved, transcendentals=flops // 1000),
    )(*args)


def student_kernel(s_ref, own, nb, gain, up, down, normed, pre, hidden, br_own, br_oth, own_in):
    xl, c, g = s_ref[1], s_ref[3], s_ref[5]
    mine = c == xl
    for b in range(2):
        for q in range(8):
            for e in range(2):
                first, second = (own, nb) if b == 0 else (nb, own)
                x = jnp.where(mine, first[e, q].astype(F32), second[e, q].astype(F32))
                mean = jnp.mean(x, axis=-1, keepdims=True)
                dev = x - mean
                var = jnp.mean(dev * dev, axis=-1, keepdims=True)
                at = 256 * b + 32 * q + 16 * e
                normed[at : at + 16, :] = (dev * lax.rsqrt(var + 1e-06) * gain[...]).astype(BF)
    x = jnp.dot(normed[...], up[...], preferred_element_type=F32)
    pre[...] = x
    k0 = math.sqrt(2 / math.pi)
    hid = (x * (0.5 * (1.0 + jnp.tanh(k0 * (x + 0.044715 * (x * x * x)))))).astype(BF)
    hidden[...] = hid
    br_own[...] = lax.dot_general(hid[0:256], down[...], NT, preferred_element_type=F32)
    br_oth[...] = lax.dot_general(hid[256:512], down[...], NT, preferred_element_type=F32)
    own_in[...] = jnp.where(mine, own[xl, g].astype(F32), nb[xl, g].astype(F32)).astype(BF)


def join_kernel(keep, own_in, out, wide):
    total = own_in[...].astype(F32)
    for k in range(16):
        total += keep[k].astype(F32)
    row = total.astype(BF)
    out[...] = row
    for k in range(16):
        wide[k] = row


def pack_kernel(own, got, out, tmp0, tmp1, tmp2, mid):
    total = own[...] + got[...]
    for t, tmp in enumerate((tmp0, tmp1, tmp2)):
        tmp[...] = total[:, 128 * t : 128 * t + 128]
        for k in range(4):
            for q in range(8):
                mid[q, 11 * k : 11 * k + 11, 128 * t : 128 * t + 128] = tmp[pl.ds(ROWS * k + q, 11, stride=8), :]
    out[...] = mid[...].astype(BF)


def add_kernel(got, out, tmp):
    total = got[0].astype(F32)
    for k in range(1, 8):
        total += got[k].astype(F32)
    tmp[...] = total
    out[...] = jnp.zeros_like(out)
    for k in range(4):
        rows = tmp[11 * k : 11 * k + 11, :]
        out[k, 0:11, :] = rows[:, 0:192]
        out[k + 4, 0:11, :] = rows[:, 192:384]


def prep_kernel(s_ref, so, *refs):
    own, far = refs[:4], refs[4:8]
    w_ref, pred_ref = refs[8:]
    y, c = s_ref[0], s_ref[3]
    for d in range(4):
        base = lax.rem(y + d, 4) * 384
        for e in range(2):
            w_ref[pl.ds(pl.multiple_of(base + 192 * e + 96 * c, 96), 96), :] = own[d][e]
            w_ref[pl.ds(pl.multiple_of(base + 192 * e + 96 * (1 - c), 96), 96), :] = far[d][e]
    pred_ref[...] = lax.dot_general(so[...], w_ref[...], NT, preferred_element_type=F32)


def head_kernel(s_ref, sums, pred, w_ref, out):
    g, c, z = s_ref[5], s_ref[3], s_ref[4]
    summed = jnp.concatenate([sums[AT[j]] for j in range(8)], axis=-1)
    row_mean = jnp.mean(summed, axis=-1, keepdims=True)
    mean_square = jnp.mean(summed * summed, axis=-1, keepdims=True)
    target = (summed - row_mean) * lax.rsqrt(mean_square - row_mean * row_mean + 1e-06)
    j = lax.broadcasted_iota(jnp.int32, (16, 1), 0)
    r = 8 * j + g
    real = (j < 11) & (r < CHUNK) & (2 * CHUNK * z + CHUNK * c + r < VALID)
    pred_grad = jnp.where(real, (pred[...] - target) * (1.0 / math.sqrt(IMAGES * VALID)), 0.0).astype(BF)
    out_grad = jnp.dot(pred_grad, w_ref[...], preferred_element_type=F32).astype(BF)
    wide = pred_grad.astype(F32)
    for k in range(8):
        for e in range(2):
            at = 192 * k + 48 * e
            out[2 * k + e, :, 0:1024] = out_grad
            cut = jnp.concatenate([wide[:, at : at + 48], wide[:, at + 96 : at + 144], jnp.zeros((16, 32), F32)], axis=-1)
            out[2 * k + e, :, 1024:1152] = cut.astype(BF)


def back_kernel(s_ref, own, far, so, hidden, pre, normed, down, out):
    c = s_ref[3]
    og = jnp.concatenate([own[:, 0:1024], far[:, 0:1024]])
    pg = jnp.concatenate([own[:, 1024:1152], far[:, 1024:1152]]).astype(F32)
    pg = jnp.where(c == 0, pg, jnp.concatenate([pg[:, 48:], pg[:, :48]], axis=-1)).astype(BF)
    head = lax.dot_general(pg, so[...], TN, preferred_element_type=F32)[0:48]
    dn = lax.dot_general(hidden[...], og, TN, preferred_element_type=F32)
    hidden_grad = jnp.dot(og, down[...], preferred_element_type=F32)
    x = pre[...]
    k0 = math.sqrt(2 / math.pi)
    t = jnp.tanh(k0 * (x + 0.044715 * (x * x * x)))
    slope = 0.5 * (1.0 + t) + 0.5 * x * (1.0 - t * t) * (k0 * (1.0 + 3 * 0.044715 * (x * x)))
    pre_grad = (hidden_grad * slope).astype(BF)
    up = lax.dot_general(pre_grad, normed[...], TN, preferred_element_type=F32)
    a = jnp.concatenate([up, head[0:24]])
    b = jnp.concatenate([dn, head[24:48]])
    low = lax.broadcasted_iota(jnp.int32, (152, 128), 1) < 64
    for k in range(8):
        at = a[:, 128 * k : 128 * k + 128]
        bt = b[:, 128 * k : 128 * k + 128]
        out[2 * k] = jnp.where(low, at, pltpu.roll(bt, 64, 1)).astype(BF)
        out[2 * k + 1] = jnp.where(low, pltpu.roll(at, 64, 1), bt).astype(BF)


def finish_kernel(got, up, down, head):
    for e in range(2):
        total = got[e].astype(F32)
        for k in range(1, 8):
            total += got[2 * k + e].astype(F32)
        t = total.T
        up[:, 128 * e : 128 * e + 128] = t[0:64, 0:128]
        down[:, 128 * e : 128 * e + 128] = t[64:128, 0:128]
        head[:, 48 * e : 48 * e + 24] = t[0:64, 128:152]
        head[:, 48 * e + 24 : 48 * e + 48] = t[64:128, 128:152]


def swap(x, axis):
    return lax.ppermute(x, axis, SWAP)


def turn(x, axis, n, by):
    return lax.ppermute(x, axis, [(k, (k - by) % n) for k in range(n)])


def spread(x, axis, n):
    x = jnp.broadcast_to(x[None], (n,) + x.shape)
    return lax.all_to_all(x, axis, 0, 0, tiled=True)


def after(x, *others):
    return lax.optimization_barrier((x,) + others)[0]


def inner(teacher_tokens, teacher_qkv, student_tokens, student_gain, w_up, w_down, w_head):
    y, xh, c, z, xl = (lax.axis_index(a) for a in ("y", "xh", "c", "z", "xl"))
    g = 2 * y + xh
    group = jnp.take(jnp.asarray(GROUP, jnp.int32), z)
    scalars = jnp.stack([y, xl, group % 3, c, z, g]).astype(jnp.int32)

    tt = lax.dynamic_slice_in_dim(teacher_tokens, y * 384, 384, 1).reshape(CHUNK, IMAGES, 384)
    rows = jnp.arange(ROWS)[:, None]
    reals = jnp.where((z == 7) & (xl == 1), VALID - 15 * CHUNK, CHUNK)

    def padded(v):
        v = jnp.pad(v, ((0, ROWS - CHUNK), (0, 0)))
        return jnp.where(rows < reals, v, v[79:80])

    mine = padded(jnp.where(xl == 0, tt[:, 0], tt[:, 1]))
    other = padded(jnp.where(xl == 0, tt[:, 1], tt[:, 0]))
    got = lax.ppermute(other, ("c", "xl"), [(0, 1), (3, 2)])
    piece = jnp.where(c == xl, mine, got)
    xa0 = spread(piece, "z", 8).reshape(8 * ROWS, 384)
    xa1 = turn(xa0, "y", 4, 1)
    xa3 = turn(xa0, "y", 4, 3)
    xa1, xa3 = lax.optimization_barrier((xa1, xa3))
    xa2 = turn(xa1[: 4 * ROWS], "y", 4, 1)
    xa2l = turn(xa3[4 * ROWS :], "y", 4, 3)
    xa = (xa0, xa1, xa2, xa2l, xa3)
    xb = tuple(swap(v, "c") for v in xa)

    wt = teacher_qkv[0].T
    main = jnp.where(xl == 0, wt[:192], wt[96:])
    part = jnp.where(xl == 0, wt[192:], wt[:96])
    to_main = [(2 * k + e, 2 * AT[(3 * k + 2 * e) % 8] + e) for k in range(8) for e in range(2)]
    to_part = [(2 * k + e, 2 * AT[(3 * k + 1) % 8] + e) for k in range(8) for e in range(2)]
    m_own = lax.ppermute(main, DP, to_main)
    h_own = lax.ppermute(part, DP, to_part)
    m_oth = swap(m_own, "xl")
    h_oth = swap(h_own, "xl")

    def arranged(v):
        v = jnp.pad(v, ((0, (128 - CHUNK) * IMAGES), (0, 0))).reshape(16, 8, IMAGES, -1)
        return v.transpose(2, 1, 0, 3)

    st_own = arranged(student_tokens)
    st_nb = swap(st_own, "xl")
    up = lax.dynamic_slice_in_dim(w_up, xl * 128, 128, 1)
    down = lax.dynamic_slice_in_dim(w_down, xl * 128, 128, 1)
    normed, pre, hidden, br_own, br_oth, own_in = call(
        student_kernel,
        [((512, 1024), BF), ((512, 128), F32), ((512, 128), BF), ((256, 1024), F32), ((256, 1024), F32), ((16, 1024), BF)],
        scalars, st_own, st_nb, student_gain[None], up, down, scalar=1, flops=300_000_000,
    )
    keep = (br_own + swap(br_oth, "c")).astype(BF).reshape(16, 16, -1)
    keep = lax.all_to_all(keep, ("y", "xh", "xl"), 0, 0, tiled=True)
    student_out, wide = call(join_kernel, [((16, 1024), BF), ((16, 16, 1024), BF)], keep, own_in)
    so_own = lax.all_to_all(wide, ("y", "xh", "xl"), 0, 0, tiled=True).reshape(256, -1)
    so_all = jnp.concatenate([so_own, swap(so_own, "c")])

    wh = w_head.T
    wh2 = swap(wh, "xh")
    pair = jnp.where(xh == 0, jnp.stack([wh, wh2]), jnp.stack([wh2, wh]))
    w_own = [pair] + [turn(pair, "y", 4, k) for k in (1, 2, 3)]
    w_far = [swap(v, "c") for v in w_own]

    t_scalars = after(scalars, student_out)
    half = 8 * ROWS
    total = 2 * half
    own, oth = call(
        teacher_kernel, [((half // 2, 384), F32)] * 2, t_scalars, *xa, *xb, m_own, m_oth, h_own, h_oth,
        scratch=[
            pltpu.VMEM((total, 1536), BF),
            pltpu.VMEM((576, 1536), BF),
            pltpu.VMEM((9, total, 64), BF),
            pltpu.VMEM((3, total, 128), BF),
        ],
        scalar=1, flops=6_000_000_000, vmem=34,
    )
    got = swap(oth, "c")
    (both,) = call(
        pack_kernel, [((8, 44, 384), BF)], own, got,
        scratch=[pltpu.VMEM((half // 2, 128), F32)] * 3 + [pltpu.VMEM((8, 44, 384), F32)],
    )
    both = after(both, so_own)
    got = lax.all_to_all(both, G, 0, 0, tiled=True)
    (sums,) = call(add_kernel, [((8, 16, 192), F32)], got, scratch=[pltpu.VMEM((44, 384), F32)])
    sums = lax.all_to_all(sums, "z", 0, 0, tiled=True)

    w_all, pred = call(
        prep_kernel, [((1536, 1024), BF), ((16, 1536), F32)], scalars, student_out, *w_own, *w_far, scalar=1
    )
    (load,) = call(head_kernel, [((16, 16, 1152), BF)], scalars, sums, pred, w_all, scalar=1)
    load = lax.all_to_all(load, ("y", "xh", "xl"), 0, 0, tiled=True).reshape(256, 1152)
    far = swap(load, "c")

    (grads,) = call(
        back_kernel, [((16, 152, 128), BF)], scalars, load, far, so_all, hidden, pre, normed, down, scalar=1
    )
    grads = lax.all_to_all(grads, DP, 0, 0, tiled=True)
    return tuple(call(finish_kernel, [((64, 256), F32), ((64, 256), F32), ((64, 96), F32)], grads))


def solution(mesh):
    fine = Mesh(mesh.devices.reshape(4, 2, 2, 8, 2), ("y", "xh", "c", "z", "xl"))
    in_specs = (
        P(DP, None),
        P(MEM, None, DP),
        P(DP, None),
        P(),
        P(None, MEM),
        P(None, MEM),
        P(None, MEM),
    )
    out_specs = (P(DP, MEM), P(DP, MEM), P(DP, MEM))
    return jax.shard_map(inner, mesh=fine, in_specs=in_specs, out_specs=out_specs, check_vma=False)
```

```python
import math

import jax
import jax.numpy as jnp
from jax import lax
from jax.experimental import pallas as pl
from jax.experimental.pallas import tpu as pltpu
from jax.sharding import Mesh, PartitionSpec as P

VALID = 1370
IMAGES = 2
BF = jnp.bfloat16
F32 = jnp.float32
MEM = ("y", "xh", "c")
DP = ("z", "xl")
GROUP = (0, 2, 1, 3, 5, 7, 4, 6)
AT = tuple(GROUP.index(j) for j in range(8))
SWAP = [(0, 1), (1, 0)]
CHUNK = 86
ROWS = 88


def teacher_kernel(s_ref, xa0, xa1, xa2, xa2l, xa3, xb0, xb1, xb2, xb2l, xb3, m_own, m_oth, h_own, h_oth, own_ref, oth_ref, xs, wt, p_sc, vx):
    y, xl, rot, c = s_ref[0], s_ref[1], s_ref[2], s_ref[3]
    half = 8 * ROWS
    total = 2 * half
    for d, (a, b) in enumerate(((xa0, xb0), (xa1, xb1), ((xa2, xa2l), (xb2, xb2l)), (xa3, xb3))):
        col = pl.multiple_of(lax.rem(y + d, 4) * 384, 384)
        if d == 2:
            for k, v in enumerate((*a, *b)):
                xs[k * half // 2 : (k + 1) * half // 2, pl.ds(col, 384)] = v[...]
        else:
            xs[0:half, pl.ds(col, 384)] = a[...]
            xs[half:total, pl.ds(col, 384)] = b[...]
    wt[pl.ds(pl.multiple_of(xl * 384, 384), 192), :] = m_own[...]
    wt[pl.ds(pl.multiple_of((1 - xl) * 384, 384), 192), :] = m_oth[...]
    wt[pl.ds(pl.multiple_of(192 + xl * 96, 96), 96), :] = h_own[...]
    wt[pl.ds(pl.multiple_of(192 + (1 - xl) * 96, 96), 96), :] = h_oth[...]
    blk = 352

    def project(i, carry):
        r0 = pl.multiple_of(i * blk, blk)
        out = lax.dot_general(xs[pl.ds(r0, blk), :], wt[...], (((1,), (1,)), ((), ())), preferred_element_type=F32).astype(BF)
        for t in range(9):
            p_sc[t, pl.ds(r0, blk), :] = out[:, 64 * t : 64 * t + 64]
        return carry

    lax.fori_loop(0, total // blk, project, 0)
    q0 = 3 * rot
    k0 = 3 * lax.rem(rot + 2, 3)
    v0 = 3 * lax.rem(rot + 1, 3)
    row = lax.broadcasted_iota(jnp.int32, (total, 1), 0)
    second = row >= half
    r = lax.rem(row, ROWS)
    zz = lax.rem(row // ROWS, 8)
    parity = jnp.where(second, 1 - c, c)
    real = r < jnp.where((zz == 7) & (parity == 1), VALID - 15 * CHUNK, CHUNK)
    realf = real.astype(F32)
    lane = lax.broadcasted_iota(jnp.int32, (total, 64), 1)
    ones = jnp.where(lane == 0, realf, 0.0).astype(BF)
    for h in range(3):
        vals = p_sc[v0 + h].astype(F32) * realf
        vx[h, :, 0:64] = vals.astype(BF)
        vx[h, :, 64:128] = ones

    for out_ref, base in ((oth_ref, half), (own_ref, 0)):
        for h in range(3):
            q = p_sc[q0 + h, pl.ds(base, half), :] * jnp.asarray(0.125, BF)
            s = lax.dot_general(q, p_sc[k0 + h], (((1,), (1,)), ((), ())), preferred_element_type=F32)
            m = jnp.max(s, axis=1, keepdims=True)
            p = jnp.exp(s - m).astype(BF)
            o = jnp.dot(p, vx[h], preferred_element_type=F32)
            context = o[:, 0:64] / o[:, 64:65]
            out_ref[:, 64 * h : 64 * h + 64] = context[0 : half // 2]
            out_ref[:, 192 + 64 * h : 256 + 64 * h] = context[half // 2 :]


VM = pl.BlockSpec(memory_space=pltpu.VMEM)
SM = pl.BlockSpec(memory_space=pltpu.SMEM)
TN = (((0,), (0,)), ((), ()))
NT = (((1,), (1,)), ((), ()))


def call(kernel, outs, *args, scratch=(), scalar=0, away=0, flops=0, vmem=24):
    shapes = [jax.ShapeDtypeStruct(s, d) for s, d in outs]
    moved = sum(math.prod(v.shape) * v.dtype.itemsize for v in args) + sum(math.prod(s.shape) * s.dtype.itemsize for s in shapes)
    return pl.pallas_call(
        kernel,
        out_shape=shapes,
        in_specs=[SM] * scalar + [pl.BlockSpec(memory_space=pltpu.HBM)] * away + [VM] * (len(args) - scalar - away),
        out_specs=[VM] * len(shapes),
        scratch_shapes=list(scratch),
        compiler_params=pltpu.CompilerParams(vmem_limit_bytes=vmem * 2**20),
        cost_estimate=pl.CostEstimate(flops=flops, bytes_accessed=moved, transcendentals=flops // 1000),
    )(*args)


def student_kernel(s_ref, own, nb, gain, up, down, normed, pre, hidden, br_own, br_oth, own_in):
    xl, c, g = s_ref[1], s_ref[3], s_ref[5]
    mine = c == xl

    @pl.loop(0, 8)
    def _(q):
        for b in range(2):
            for e in range(2):
                first, second = (own, nb) if b == 0 else (nb, own)
                x = jnp.where(mine, first[e, q].astype(F32), second[e, q].astype(F32))
                mean = jnp.mean(x, axis=-1, keepdims=True)
                dev = x - mean
                var = jnp.mean(dev * dev, axis=-1, keepdims=True)
                at = pl.multiple_of(256 * b + 32 * q + 16 * e, 16)
                normed[pl.ds(at, 16), :] = (dev * lax.rsqrt(var + 1e-06) * gain[...]).astype(BF)

    x = jnp.dot(normed[...], up[...], preferred_element_type=F32)
    pre[...] = x
    k0 = math.sqrt(2 / math.pi)
    hid = (x * (0.5 * (1.0 + jnp.tanh(k0 * (x + 0.044715 * (x * x * x)))))).astype(BF)
    hidden[...] = hid
    br_own[...] = lax.dot_general(hid[0:256], down[...], NT, preferred_element_type=F32)
    br_oth[...] = lax.dot_general(hid[256:512], down[...], NT, preferred_element_type=F32).astype(BF)
    own_in[...] = jnp.where(mine, own[xl, g].astype(F32), nb[xl, g].astype(F32)).astype(BF)


def join_kernel(keep, own_in, out, wide):
    total = own_in[...].astype(F32)
    for k in range(16):
        total += keep[k].astype(F32)
    row = total.astype(BF)
    out[...] = row
    for k in range(16):
        wide[k] = row


def pair_kernel(s_ref, own, other, out):
    xh = lax.rem(s_ref[5], 2)
    out[xh] = own[...]
    out[1 - xh] = other[...]


def branch_kernel(own, got, out):
    out[...] = (own[...] + got[...].astype(F32)).astype(BF)


def pack_kernel(own, got, out, a0, a1, b0, b1, mid):
    total = own[...] + got[...]
    a0[...] = total[:, 0:128]
    a1[:, 0:64] = total[:, 128:192]
    b0[...] = total[:, 192:320]
    b1[:, 0:64] = total[:, 320:384]
    mid[...] = jnp.zeros_like(mid)

    @pl.loop(0, 8)
    def _(q):
        for k in range(8):
            first, second = (a0, a1) if k < 4 else (b0, b1)
            at = ROWS * (k % 4) + q
            to = 8 * q + k
            mid[to, :, 0:128] = first[pl.ds(at, 8, stride=8), :]
            mid[to, :, 128:192] = second[pl.ds(at, 8, stride=8), :][:, 0:64]
            mid[to, 0:3, 192:320] = first[pl.ds(at + 64, 3, stride=8), :]
            mid[to, 0:3, 320:384] = second[pl.ds(at + 64, 3, stride=8), :][:, 0:64]

    out[...] = mid[...].astype(BF)


def prep_kernel(s_ref, so, *refs):
    own, far = refs[:4], refs[4:8]
    w_ref, pred_ref = refs[8:]
    y, c = s_ref[0], s_ref[3]
    for d in range(4):
        base = lax.rem(y + d, 4) * 384
        for e in range(2):
            w_ref[pl.ds(pl.multiple_of(base + 192 * e + 96 * c, 96), 96), :] = own[d][e]
            w_ref[pl.ds(pl.multiple_of(base + 192 * e + 96 * (1 - c), 96), 96), :] = far[d][e]
    pred_ref[...] = lax.dot_general(so[...], w_ref[...], NT, preferred_element_type=F32)


def head_kernel(s_ref, w_hbm, sums, pred, out, w_ref, sem):
    copy = pltpu.make_async_copy(w_hbm, w_ref, sem)
    copy.start()
    g, c, z = s_ref[5], s_ref[3], s_ref[4]
    parts = []
    for k in range(8):
        total = sums[k].astype(F32)
        for m in range(1, 8):
            total += sums[8 * m + k].astype(F32)
        parts.append(jnp.concatenate([total[:, 0:192], total[:, 192:384]]))
    summed = jnp.concatenate([parts[AT[j]] for j in range(8)], axis=-1)
    row_mean = jnp.mean(summed, axis=-1, keepdims=True)
    mean_square = jnp.mean(summed * summed, axis=-1, keepdims=True)
    target = (summed - row_mean) * lax.rsqrt(mean_square - row_mean * row_mean + 1e-06)
    j = lax.broadcasted_iota(jnp.int32, (16, 1), 0)
    r = 8 * j + g
    real = (j < 11) & (r < CHUNK) & (2 * CHUNK * z + CHUNK * c + r < VALID)
    pred_grad = jnp.where(real, (pred[...] - target) * (1.0 / math.sqrt(IMAGES * VALID)), 0.0).astype(BF)
    copy.wait()
    out_grad = jnp.dot(pred_grad, w_ref[...], preferred_element_type=F32).astype(BF)
    wide = pred_grad.astype(F32)
    for k in range(8):
        for e in range(2):
            at = 192 * k + 48 * e
            out[2 * k + e, :, 0:1024] = out_grad
            cut = jnp.concatenate([wide[:, at : at + 48], wide[:, at + 96 : at + 144], jnp.zeros((16, 32), F32)], axis=-1)
            out[2 * k + e, :, 1024:1152] = cut.astype(BF)


def back_kernel(s_ref, own, far, so, so_far, hidden, pre, normed, down, out):
    c = s_ref[3]
    og = jnp.concatenate([own[:, 0:1024], far[:, 0:1024]])
    pg = jnp.concatenate([own[:, 1024:1152], far[:, 1024:1152]]).astype(F32)
    pg = jnp.where(c == 0, pg, jnp.concatenate([pg[:, 48:], pg[:, :48]], axis=-1)).astype(BF)
    head = lax.dot_general(pg, jnp.concatenate([so[...], so_far[...]]), TN, preferred_element_type=F32)[0:48]
    dn = lax.dot_general(hidden[...], og, TN, preferred_element_type=F32)
    hidden_grad = jnp.dot(og, down[...], preferred_element_type=F32)
    x = pre[...]
    k0 = math.sqrt(2 / math.pi)
    t = jnp.tanh(k0 * (x + 0.044715 * (x * x * x)))
    slope = 0.5 * (1.0 + t) + 0.5 * x * (1.0 - t * t) * (k0 * (1.0 + 3 * 0.044715 * (x * x)))
    pre_grad = (hidden_grad * slope).astype(BF)
    up = lax.dot_general(pre_grad, normed[...], TN, preferred_element_type=F32)
    a = jnp.concatenate([up, head[0:24]])
    b = jnp.concatenate([dn, head[24:48]])
    low = lax.broadcasted_iota(jnp.int32, (152, 128), 1) < 64
    for k in range(8):
        at = a[:, 128 * k : 128 * k + 128]
        bt = b[:, 128 * k : 128 * k + 128]
        out[2 * k] = jnp.where(low, at, pltpu.roll(bt, 64, 1)).astype(BF)
        out[2 * k + 1] = jnp.where(low, pltpu.roll(at, 64, 1), bt).astype(BF)


def finish_kernel(got, up, down, head):
    for e in range(2):
        total = got[e].astype(F32)
        for k in range(1, 8):
            total += got[2 * k + e].astype(F32)
        t = total.T
        up[:, 128 * e : 128 * e + 128] = t[0:64, 0:128]
        down[:, 128 * e : 128 * e + 128] = t[64:128, 0:128]
        head[:, 48 * e : 48 * e + 24] = t[0:64, 128:152]
        head[:, 48 * e + 24 : 48 * e + 48] = t[64:128, 128:152]


def swap(x, axis):
    return lax.ppermute(x, axis, SWAP)


def turn(x, axis, n, by):
    return lax.ppermute(x, axis, [(k, (k - by) % n) for k in range(n)])


def spread(x, axis, n):
    x = jnp.broadcast_to(x[None], (n,) + x.shape)
    return lax.all_to_all(x, axis, 0, 0, tiled=True)


def after(x, *others):
    return lax.optimization_barrier((x,) + others)[0]


def inner(teacher_tokens, teacher_qkv, student_tokens, student_gain, w_up, w_down, w_head):
    y, xh, c, z, xl = (lax.axis_index(a) for a in ("y", "xh", "c", "z", "xl"))
    g = 2 * y + xh
    group = jnp.take(jnp.asarray(GROUP, jnp.int32), z)
    scalars = jnp.stack([y, xl, group % 3, c, z, g]).astype(jnp.int32)

    tt = lax.dynamic_slice_in_dim(teacher_tokens, y * 384, 384, 1).reshape(CHUNK, IMAGES, 384)
    rows = jnp.arange(ROWS)[:, None]
    reals = jnp.where((z == 7) & (xl == 1), VALID - 15 * CHUNK, CHUNK)

    def padded(v):
        v = jnp.pad(v, ((0, ROWS - CHUNK), (0, 0)))
        return jnp.where(rows < reals, v, v[79:80])

    mine = padded(jnp.where(xl == 0, tt[:, 0], tt[:, 1]))
    other = padded(jnp.where(xl == 0, tt[:, 1], tt[:, 0]))
    got = lax.ppermute(other, ("c", "xl"), [(0, 1), (3, 2)])
    piece = jnp.where(c == xl, mine, got)
    xa0 = spread(piece, "z", 8).reshape(8 * ROWS, 384)
    xa1 = turn(xa0, "y", 4, 1)
    xa3 = turn(xa0, "y", 4, 3)
    xa1, xa3 = lax.optimization_barrier((xa1, xa3))
    xa2 = turn(xa1[: 4 * ROWS], "y", 4, 1)
    xa2l = turn(xa3[4 * ROWS :], "y", 4, 3)
    xa = (xa0, xa1, xa2, xa2l, xa3)
    xb = tuple(swap(v, "c") for v in xa)

    wt = teacher_qkv[0].T
    main = jnp.where(xl == 0, wt[:192], wt[96:])
    part = jnp.where(xl == 0, wt[192:], wt[:96])
    to_main = [(2 * k + e, 2 * AT[(3 * k + 2 * e) % 8] + e) for k in range(8) for e in range(2)]
    to_part = [(2 * k + e, 2 * AT[(3 * k + 1) % 8] + e) for k in range(8) for e in range(2)]
    m_own = lax.ppermute(main, DP, to_main)
    h_own = lax.ppermute(part, DP, to_part)
    m_oth = swap(m_own, "xl")
    h_oth = swap(h_own, "xl")

    def arranged(v):
        v = jnp.pad(v, ((0, (128 - CHUNK) * IMAGES), (0, 0))).reshape(16, 8, IMAGES, -1)
        return v.transpose(2, 1, 0, 3)

    st_own = arranged(student_tokens)
    st_nb = swap(st_own, "xl")
    up = lax.dynamic_slice_in_dim(w_up, xl * 128, 128, 1)
    down = lax.dynamic_slice_in_dim(w_down, xl * 128, 128, 1)
    normed, pre, hidden, br_own, br_oth, own_in = call(
        student_kernel,
        [((512, 1024), BF), ((512, 128), F32), ((512, 128), BF), ((256, 1024), F32), ((256, 1024), BF), ((16, 1024), BF)],
        scalars, st_own, st_nb, student_gain[None], up, down, scalar=1, flops=300_000_000,
    )
    (keep,) = call(branch_kernel, [((256, 1024), BF)], br_own, swap(br_oth, "c"))
    keep = keep.reshape(16, 16, -1)
    keep = lax.all_to_all(keep, ("y", "xh", "xl"), 0, 0, tiled=True)
    student_out, wide = call(join_kernel, [((16, 1024), BF), ((16, 16, 1024), BF)], keep, own_in)
    so_own = lax.all_to_all(wide, ("y", "xh", "xl"), 0, 0, tiled=True).reshape(256, -1)
    so_far = swap(so_own, "c")

    wh = w_head.T
    wh2 = swap(wh, "xh")
    (pair,) = call(pair_kernel, [((2, 96, 1024), BF)], scalars, wh, wh2, scalar=1)
    w_own = [pair] + [turn(pair, "y", 4, k) for k in (1, 2, 3)]
    w_far = [swap(v, "c") for v in w_own]

    t_scalars = after(scalars, student_out)
    half = 8 * ROWS
    total = 2 * half
    own, oth = call(
        teacher_kernel, [((half // 2, 384), F32)] * 2, t_scalars, *xa, *xb, m_own, m_oth, h_own, h_oth,
        scratch=[
            pltpu.VMEM((total, 1536), BF),
            pltpu.VMEM((576, 1536), BF),
            pltpu.VMEM((9, total, 64), BF),
            pltpu.VMEM((3, total, 128), BF),
        ],
        scalar=1, flops=6_000_000_000, vmem=34,
    )
    got = swap(oth, "c")
    (both,) = call(
        pack_kernel, [((64, 8, 384), BF)], own, got,
        scratch=[pltpu.VMEM((half // 2, 128), F32)] * 4 + [pltpu.VMEM((64, 8, 384), F32)],
    )
    both = after(both, so_own)
    sums = lax.all_to_all(both, ("y", "xh", "z"), 0, 0, tiled=True)

    w_all, pred = call(
        prep_kernel, [((1536, 1024), BF), ((16, 1536), F32)], scalars, student_out, *w_own, *w_far, scalar=1
    )
    (load,) = call(
        head_kernel, [((16, 16, 1152), BF)], scalars, w_all, sums, pred,
        scratch=[pltpu.VMEM((1536, 1024), BF), pltpu.SemaphoreType.DMA], scalar=1, away=1, vmem=58,
    )
    load = lax.all_to_all(load, ("y", "xh", "xl"), 0, 0, tiled=True).reshape(256, 1152)
    far = swap(load, "c")

    (grads,) = call(
        back_kernel, [((16, 152, 128), BF)], scalars, load, far, so_own, so_far, hidden, pre, normed, down, scalar=1
    )
    grads = lax.all_to_all(grads, DP, 0, 0, tiled=True)
    return tuple(call(finish_kernel, [((64, 256), F32), ((64, 256), F32), ((64, 96), F32)], grads))


def solution(mesh):
    fine = Mesh(mesh.devices.reshape(4, 2, 2, 8, 2), ("y", "xh", "c", "z", "xl"))
    in_specs = (
        P(DP, None),
        P(MEM, None, DP),
        P(DP, None),
        P(),
        P(None, MEM),
        P(None, MEM),
        P(None, MEM),
    )
    out_specs = (P(DP, MEM), P(DP, MEM), P(DP, MEM))
    return jax.shard_map(inner, mesh=fine, in_specs=in_specs, out_specs=out_specs, check_vma=False)
```

```python
import math

import jax
import jax.numpy as jnp
from jax import lax
from jax.experimental import pallas as pl
from jax.experimental.pallas import tpu as pltpu
from jax.sharding import Mesh, PartitionSpec as P

VALID = 1370
IMAGES = 2
BF = jnp.bfloat16
F32 = jnp.float32
MEM = ("y", "xh", "c")
DP = ("z", "xl")
GROUP = (0, 2, 1, 3, 5, 7, 4, 6)
AT = tuple(GROUP.index(j) for j in range(8))
SWAP = [(0, 1), (1, 0)]
CHUNK = 86
ROWS = 88


def teacher_kernel(s_ref, xa0, xa1, xa2, xa2l, xa3, xb0, xb1, xb2, xb2l, xb3, m_own, m_oth, h_own, h_oth, own_ref, oth_ref, xs, wt, p_sc, vx):
    y, xl, rot, c = s_ref[0], s_ref[1], s_ref[2], s_ref[3]
    half = 8 * ROWS
    total = 2 * half
    for d, (a, b) in enumerate(((xa0, xb0), (xa1, xb1), ((xa2, xa2l), (xb2, xb2l)), (xa3, xb3))):
        col = pl.multiple_of(lax.rem(y + d, 4) * 384, 384)
        if d == 2:
            for k, v in enumerate((*a, *b)):
                xs[k * half // 2 : (k + 1) * half // 2, pl.ds(col, 384)] = v[...]
        else:
            xs[0:half, pl.ds(col, 384)] = a[...]
            xs[half:total, pl.ds(col, 384)] = b[...]
    wt[pl.ds(pl.multiple_of(xl * 384, 384), 192), :] = m_own[...]
    wt[pl.ds(pl.multiple_of((1 - xl) * 384, 384), 192), :] = m_oth[...]
    wt[pl.ds(pl.multiple_of(192 + xl * 96, 96), 96), :] = h_own[...]
    wt[pl.ds(pl.multiple_of(192 + (1 - xl) * 96, 96), 96), :] = h_oth[...]
    blk = 352

    def project(i, carry):
        r0 = pl.multiple_of(i * blk, blk)
        out = lax.dot_general(xs[pl.ds(r0, blk), :], wt[...], (((1,), (1,)), ((), ())), preferred_element_type=F32).astype(BF)
        for t in range(9):
            p_sc[t, pl.ds(r0, blk), :] = out[:, 64 * t : 64 * t + 64]
        return carry

    lax.fori_loop(0, total // blk, project, 0)
    q0 = 3 * rot
    k0 = 3 * lax.rem(rot + 2, 3)
    v0 = 3 * lax.rem(rot + 1, 3)
    row = lax.broadcasted_iota(jnp.int32, (total, 1), 0)
    second = row >= half
    r = lax.rem(row, ROWS)
    zz = lax.rem(row // ROWS, 8)
    parity = jnp.where(second, 1 - c, c)
    real = r < jnp.where((zz == 7) & (parity == 1), VALID - 15 * CHUNK, CHUNK)
    realf = real.astype(F32)
    lane = lax.broadcasted_iota(jnp.int32, (total, 64), 1)
    ones = jnp.where(lane == 0, realf, 0.0).astype(BF)
    for h in range(3):
        vals = p_sc[v0 + h].astype(F32) * realf
        vx[h, :, 0:64] = vals.astype(BF)
        vx[h, :, 64:128] = ones

    for out_ref, base in ((oth_ref, half), (own_ref, 0)):
        for h in range(3):
            q = p_sc[q0 + h, pl.ds(base, half), :] * jnp.asarray(0.125, BF)
            s = lax.dot_general(q, p_sc[k0 + h], (((1,), (1,)), ((), ())), preferred_element_type=F32)
            m = jnp.max(s, axis=1, keepdims=True)
            p = jnp.exp(s - m).astype(BF)
            o = jnp.dot(p, vx[h], preferred_element_type=F32)
            context = o[:, 0:64] / o[:, 64:65]
            out_ref[:, 64 * h : 64 * h + 64] = context[0 : half // 2]
            out_ref[:, 192 + 64 * h : 256 + 64 * h] = context[half // 2 :]


VM = pl.BlockSpec(memory_space=pltpu.VMEM)
SM = pl.BlockSpec(memory_space=pltpu.SMEM)
TN = (((0,), (0,)), ((), ()))
NT = (((1,), (1,)), ((), ()))


def call(kernel, outs, *args, scratch=(), scalar=0, away=0, flops=0, vmem=24):
    shapes = [jax.ShapeDtypeStruct(s, d) for s, d in outs]
    moved = sum(math.prod(v.shape) * v.dtype.itemsize for v in args) + sum(math.prod(s.shape) * s.dtype.itemsize for s in shapes)
    return pl.pallas_call(
        kernel,
        out_shape=shapes,
        in_specs=[SM] * scalar + [pl.BlockSpec(memory_space=pltpu.HBM)] * away + [VM] * (len(args) - scalar - away),
        out_specs=[VM] * len(shapes),
        scratch_shapes=list(scratch),
        compiler_params=pltpu.CompilerParams(vmem_limit_bytes=vmem * 2**20),
        cost_estimate=pl.CostEstimate(flops=flops, bytes_accessed=moved, transcendentals=flops // 1000),
    )(*args)


def student_kernel(s_ref, own, nb, gain, up, down, normed, pre, hidden, br_own, br_oth, own_in):
    xl, c, g = s_ref[1], s_ref[3], s_ref[5]
    mine = c == xl

    @pl.loop(0, 8)
    def _(q):
        for b in range(2):
            for e in range(2):
                first, second = (own, nb) if b == 0 else (nb, own)
                x = jnp.where(mine, first[e, q].astype(F32), second[e, q].astype(F32))
                mean = jnp.mean(x, axis=-1, keepdims=True)
                dev = x - mean
                var = jnp.mean(dev * dev, axis=-1, keepdims=True)
                at = pl.multiple_of(256 * b + 32 * q + 16 * e, 16)
                normed[pl.ds(at, 16), :] = (dev * lax.rsqrt(var + 1e-06) * gain[...]).astype(BF)

    x = jnp.dot(normed[...], up[...], preferred_element_type=F32)
    pre[...] = x
    k0 = math.sqrt(2 / math.pi)
    hid = (x * (0.5 * (1.0 + jnp.tanh(k0 * (x + 0.044715 * (x * x * x)))))).astype(BF)
    hidden[...] = hid
    br_own[...] = lax.dot_general(hid[0:256], down[...], NT, preferred_element_type=F32)
    br_oth[...] = lax.dot_general(hid[256:512], down[...], NT, preferred_element_type=F32).astype(BF)
    own_in[...] = jnp.where(mine, own[xl, g].astype(F32), nb[xl, g].astype(F32)).astype(BF)


def join_kernel(keep, own_in, out, wide):
    total = own_in[...].astype(F32)
    for k in range(16):
        total += keep[k].astype(F32)
    row = total.astype(BF)
    out[...] = row
    for k in range(16):
        wide[k] = row


def pair_kernel(s_ref, own, other, out):
    xh = lax.rem(s_ref[5], 2)
    out[xh] = own[...]
    out[1 - xh] = other[...]


def branch_kernel(own, got, out):
    out[...] = (own[...] + got[...].astype(F32)).astype(BF)


def pack_kernel(own, got, out, a0, a1, b0, b1, mid):
    total = own[...] + got[...]
    a0[...] = total[:, 0:128]
    a1[:, 0:64] = total[:, 128:192]
    b0[...] = total[:, 192:320]
    b1[:, 0:64] = total[:, 320:384]
    mid[...] = jnp.zeros_like(mid)

    @pl.loop(0, 8)
    def _(q):
        for k in range(8):
            first, second = (a0, a1) if k < 4 else (b0, b1)
            at = ROWS * (k % 4) + q
            to = 8 * q + k
            mid[to, :, 0:128] = first[pl.ds(at, 8, stride=8), :]
            mid[to, :, 128:192] = second[pl.ds(at, 8, stride=8), :][:, 0:64]
            mid[to, 0:3, 192:320] = first[pl.ds(at + 64, 3, stride=8), :]
            mid[to, 0:3, 320:384] = second[pl.ds(at + 64, 3, stride=8), :][:, 0:64]

    out[...] = mid[...].astype(BF)


def prep_kernel(s_ref, so, *refs):
    own, far = refs[:4], refs[4:8]
    w_ref, pred_ref = refs[8:]
    y, c = s_ref[0], s_ref[3]
    for d in range(4):
        base = lax.rem(y + d, 4) * 384
        for e in range(2):
            w_ref[pl.ds(pl.multiple_of(base + 192 * e + 96 * c, 96), 96), :] = own[d][e]
            w_ref[pl.ds(pl.multiple_of(base + 192 * e + 96 * (1 - c), 96), 96), :] = far[d][e]
    pred_ref[...] = lax.dot_general(so[...], w_ref[...], NT, preferred_element_type=F32)


def head_kernel(s_ref, w_hbm, sums, pred, out, w_ref, sem):
    copy = pltpu.make_async_copy(w_hbm, w_ref, sem)
    copy.start()
    g, c, z = s_ref[5], s_ref[3], s_ref[4]
    parts = []
    for k in range(8):
        total = sums[k].astype(F32)
        for m in range(1, 8):
            total += sums[8 * m + k].astype(F32)
        parts.append(jnp.concatenate([total[:, 0:192], total[:, 192:384]]))
    summed = jnp.concatenate([parts[AT[j]] for j in range(8)], axis=-1)
    row_mean = jnp.mean(summed, axis=-1, keepdims=True)
    mean_square = jnp.mean(summed * summed, axis=-1, keepdims=True)
    target = (summed - row_mean) * lax.rsqrt(mean_square - row_mean * row_mean + 1e-06)
    j = lax.broadcasted_iota(jnp.int32, (16, 1), 0)
    r = 8 * j + g
    real = (j < 11) & (r < CHUNK) & (2 * CHUNK * z + CHUNK * c + r < VALID)
    pred_grad = jnp.where(real, (pred[...] - target) * (1.0 / math.sqrt(IMAGES * VALID)), 0.0).astype(BF)
    copy.wait()
    out_grad = jnp.dot(pred_grad, w_ref[...], preferred_element_type=F32).astype(BF)
    wide = pred_grad.astype(F32)
    for k in range(8):
        for e in range(2):
            at = 192 * k + 48 * e
            out[2 * k + e, :, 0:1024] = out_grad
            cut = jnp.concatenate([wide[:, at : at + 48], wide[:, at + 96 : at + 144], jnp.zeros((16, 32), F32)], axis=-1)
            out[2 * k + e, :, 1024:1152] = cut.astype(BF)


def back_kernel(s_ref, own, far, so, so_far, hidden, pre, normed, down, out):
    c = s_ref[3]
    og = jnp.concatenate([own[:, 0:1024], far[:, 0:1024]])
    pg = jnp.concatenate([own[:, 1024:1152], far[:, 1024:1152]]).astype(F32)
    pg = jnp.where(c == 0, pg, jnp.concatenate([pg[:, 48:], pg[:, :48]], axis=-1)).astype(BF)
    head = lax.dot_general(pg, jnp.concatenate([so[...], so_far[...]]), TN, preferred_element_type=F32)[0:48]
    dn = lax.dot_general(hidden[...], og, TN, preferred_element_type=F32)
    hidden_grad = jnp.dot(og, down[...], preferred_element_type=F32)
    x = pre[...]
    k0 = math.sqrt(2 / math.pi)
    t = jnp.tanh(k0 * (x + 0.044715 * (x * x * x)))
    slope = 0.5 * (1.0 + t) + 0.5 * x * (1.0 - t * t) * (k0 * (1.0 + 3 * 0.044715 * (x * x)))
    pre_grad = (hidden_grad * slope).astype(BF)
    up = lax.dot_general(pre_grad, normed[...], TN, preferred_element_type=F32)
    a = jnp.concatenate([up, head[0:24]])
    b = jnp.concatenate([dn, head[24:48]])
    low = lax.broadcasted_iota(jnp.int32, (152, 128), 1) < 64
    for k in range(8):
        at = a[:, 128 * k : 128 * k + 128]
        bt = b[:, 128 * k : 128 * k + 128]
        out[2 * k] = jnp.where(low, at, pltpu.roll(bt, 64, 1)).astype(BF)
        out[2 * k + 1] = jnp.where(low, pltpu.roll(at, 64, 1), bt).astype(BF)


def finish_kernel(got, up, down, head):
    for e in range(2):
        total = got[e].astype(F32)
        for k in range(1, 8):
            total += got[2 * k + e].astype(F32)
        t = total.T
        up[:, 128 * e : 128 * e + 128] = t[0:64, 0:128]
        down[:, 128 * e : 128 * e + 128] = t[64:128, 0:128]
        head[:, 48 * e : 48 * e + 24] = t[0:64, 128:152]
        head[:, 48 * e + 24 : 48 * e + 48] = t[64:128, 128:152]


def halves_kernel(a, b, top, low):
    top[...] = a[...]
    low[...] = b[...]


def halves(a, b):
    shape = (a.shape[0] // 2, a.shape[1])
    first = pl.BlockSpec(shape, lambda i: (0, 0))
    return pl.pallas_call(
        halves_kernel,
        grid=(1,),
        out_shape=[jax.ShapeDtypeStruct(shape, a.dtype)] * 2,
        in_specs=[first, pl.BlockSpec(shape, lambda i: (1, 0))],
        out_specs=[first, first],
        name="halves",
    )(a, b)


def swap(x, axis):
    return lax.ppermute(x, axis, SWAP)


def turn(x, axis, n, by):
    return lax.ppermute(x, axis, [(k, (k - by) % n) for k in range(n)])


def spread(x, axis, n):
    x = jnp.broadcast_to(x[None], (n,) + x.shape)
    return lax.all_to_all(x, axis, 0, 0, tiled=True)


def after(x, *others):
    return lax.optimization_barrier((x,) + others)[0]


def inner(teacher_tokens, teacher_qkv, student_tokens, student_gain, w_up, w_down, w_head):
    y, xh, c, z, xl = (lax.axis_index(a) for a in ("y", "xh", "c", "z", "xl"))
    g = 2 * y + xh
    group = jnp.take(jnp.asarray(GROUP, jnp.int32), z)
    scalars = jnp.stack([y, xl, group % 3, c, z, g]).astype(jnp.int32)

    tt = lax.dynamic_slice_in_dim(teacher_tokens, y * 384, 384, 1).reshape(CHUNK, IMAGES, 384)
    rows = jnp.arange(ROWS)[:, None]
    reals = jnp.where((z == 7) & (xl == 1), VALID - 15 * CHUNK, CHUNK)

    def padded(v):
        v = jnp.pad(v, ((0, ROWS - CHUNK), (0, 0)))
        return jnp.where(rows < reals, v, v[79:80])

    mine = padded(jnp.where(xl == 0, tt[:, 0], tt[:, 1]))
    other = padded(jnp.where(xl == 0, tt[:, 1], tt[:, 0]))
    got = lax.ppermute(other, ("c", "xl"), [(0, 1), (3, 2)])
    piece = jnp.where(c == xl, mine, got)
    xa0 = spread(piece, "z", 8).reshape(8 * ROWS, 384)
    xa1 = turn(xa0, "y", 4, 1)
    xa3 = turn(xa0, "y", 4, 3)
    top, low = halves(xa1, xa3)
    xa2 = turn(top, "y", 4, 1)
    xa2l = turn(low, "y", 4, 3)
    xa = (xa0, xa1, xa2, xa2l, xa3)
    xb = tuple(swap(v, "c") for v in xa)

    wt = teacher_qkv[0].T
    main = jnp.where(xl == 0, wt[:192], wt[96:])
    part = jnp.where(xl == 0, wt[192:], wt[:96])
    to_main = [(2 * k + e, 2 * AT[(3 * k + 2 * e) % 8] + e) for k in range(8) for e in range(2)]
    to_part = [(2 * k + e, 2 * AT[(3 * k + 1) % 8] + e) for k in range(8) for e in range(2)]
    m_own = lax.ppermute(main, DP, to_main)
    h_own = lax.ppermute(part, DP, to_part)
    m_oth = swap(m_own, "xl")
    h_oth = swap(h_own, "xl")

    def arranged(v):
        v = jnp.pad(v, ((0, (128 - CHUNK) * IMAGES), (0, 0))).reshape(16, 8, IMAGES, -1)
        return v.transpose(2, 1, 0, 3)

    st_own = arranged(student_tokens)
    st_nb = swap(st_own, "xl")
    up = lax.dynamic_slice_in_dim(w_up, xl * 128, 128, 1)
    down = lax.dynamic_slice_in_dim(w_down, xl * 128, 128, 1)
    normed, pre, hidden, br_own, br_oth, own_in = call(
        student_kernel,
        [((512, 1024), BF), ((512, 128), F32), ((512, 128), BF), ((256, 1024), F32), ((256, 1024), BF), ((16, 1024), BF)],
        scalars, st_own, st_nb, student_gain[None], up, down, scalar=1, flops=300_000_000,
    )
    (keep,) = call(branch_kernel, [((256, 1024), BF)], br_own, swap(br_oth, "c"))
    keep = keep.reshape(16, 16, -1)
    keep = lax.all_to_all(keep, ("y", "xh", "xl"), 0, 0, tiled=True)
    student_out, wide = call(join_kernel, [((16, 1024), BF), ((16, 16, 1024), BF)], keep, own_in)
    so_own = lax.all_to_all(wide, ("y", "xh", "xl"), 0, 0, tiled=True).reshape(256, -1)
    so_far = swap(so_own, "c")

    wh = w_head.T
    wh2 = swap(wh, "xh")
    (pair,) = call(pair_kernel, [((2, 96, 1024), BF)], scalars, wh, wh2, scalar=1)
    w_own = [pair] + [turn(pair, "y", 4, k) for k in (1, 2, 3)]
    w_far = [swap(v, "c") for v in w_own]

    t_scalars = after(scalars, student_out)
    half = 8 * ROWS
    total = 2 * half
    own, oth = call(
        teacher_kernel, [((half // 2, 384), F32)] * 2, t_scalars, *xa, *xb, m_own, m_oth, h_own, h_oth,
        scratch=[
            pltpu.VMEM((total, 1536), BF),
            pltpu.VMEM((576, 1536), BF),
            pltpu.VMEM((9, total, 64), BF),
            pltpu.VMEM((3, total, 128), BF),
        ],
        scalar=1, flops=6_000_000_000, vmem=34,
    )
    got = swap(oth, "c")
    (both,) = call(
        pack_kernel, [((64, 8, 384), BF)], own, got,
        scratch=[pltpu.VMEM((half // 2, 128), F32)] * 4 + [pltpu.VMEM((64, 8, 384), F32)],
    )
    both = after(both, so_own)
    sums = lax.all_to_all(both, ("y", "xh", "z"), 0, 0, tiled=True)

    w_all, pred = call(
        prep_kernel, [((1536, 1024), BF), ((16, 1536), F32)], scalars, student_out, *w_own, *w_far, scalar=1
    )
    (load,) = call(
        head_kernel, [((16, 16, 1152), BF)], scalars, w_all, sums, pred,
        scratch=[pltpu.VMEM((1536, 1024), BF), pltpu.SemaphoreType.DMA], scalar=1, away=1, vmem=58,
    )
    load = lax.all_to_all(load, ("y", "xh", "xl"), 0, 0, tiled=True).reshape(256, 1152)
    far = swap(load, "c")

    (grads,) = call(
        back_kernel, [((16, 152, 128), BF)], scalars, load, far, so_own, so_far, hidden, pre, normed, down, scalar=1
    )
    grads = lax.all_to_all(grads, DP, 0, 0, tiled=True)
    return tuple(call(finish_kernel, [((64, 256), F32), ((64, 256), F32), ((64, 96), F32)], grads))


def solution(mesh):
    fine = Mesh(mesh.devices.reshape(4, 2, 2, 8, 2), ("y", "xh", "c", "z", "xl"))
    in_specs = (
        P(DP, None),
        P(MEM, None, DP),
        P(DP, None),
        P(),
        P(None, MEM),
        P(None, MEM),
        P(None, MEM),
    )
    out_specs = (P(DP, MEM), P(DP, MEM), P(DP, MEM))
    return jax.shard_map(inner, mesh=fine, in_specs=in_specs, out_specs=out_specs, check_vma=False)
```

```python
import math

import jax
import jax.numpy as jnp
from jax import lax
from jax.experimental import pallas as pl
from jax.experimental.pallas import tpu as pltpu
from jax.sharding import Mesh, PartitionSpec as P

VALID = 1370
IMAGES = 2
BF = jnp.bfloat16
F32 = jnp.float32
MEM = ("y", "xh", "c")
DP = ("z", "xl")
GROUP = (0, 2, 1, 3, 5, 7, 4, 6)
AT = tuple(GROUP.index(j) for j in range(8))
SWAP = [(0, 1), (1, 0)]
CHUNK = 86
ROWS = 88


def teacher_kernel(s_ref, xa0, xa1, xa2, xa2l, xa3, xb0, xb1, xb2, xb2l, xb3, m_own, m_oth, h_own, h_oth, own_ref, oth_ref, xs, wt, p_sc, vx):
    y, xl, rot, c = s_ref[0], s_ref[1], s_ref[2], s_ref[3]
    half = 8 * ROWS
    total = 2 * half
    for d, (a, b) in enumerate(((xa0, xb0), (xa1, xb1), ((xa2, xa2l), (xb2, xb2l)), (xa3, xb3))):
        col = pl.multiple_of(lax.rem(y + d, 4) * 384, 384)
        if d == 2:
            for k, v in enumerate((*a, *b)):
                xs[k * half // 2 : (k + 1) * half // 2, pl.ds(col, 384)] = v[...]
        else:
            xs[0:half, pl.ds(col, 384)] = a[...]
            xs[half:total, pl.ds(col, 384)] = b[...]
    wt[pl.ds(pl.multiple_of(xl * 384, 384), 192), :] = m_own[...]
    wt[pl.ds(pl.multiple_of((1 - xl) * 384, 384), 192), :] = m_oth[...]
    wt[pl.ds(pl.multiple_of(192 + xl * 96, 96), 96), :] = h_own[...]
    wt[pl.ds(pl.multiple_of(192 + (1 - xl) * 96, 96), 96), :] = h_oth[...]
    blk = 352

    def project(i, carry):
        r0 = pl.multiple_of(i * blk, blk)
        out = lax.dot_general(xs[pl.ds(r0, blk), :], wt[...], (((1,), (1,)), ((), ())), preferred_element_type=F32).astype(BF)
        for t in range(9):
            p_sc[t, pl.ds(r0, blk), :] = out[:, 64 * t : 64 * t + 64]
        return carry

    lax.fori_loop(0, total // blk, project, 0)
    q0 = 3 * rot
    k0 = 3 * lax.rem(rot + 2, 3)
    v0 = 3 * lax.rem(rot + 1, 3)
    row = lax.broadcasted_iota(jnp.int32, (total, 1), 0)
    second = row >= half
    r = lax.rem(row, ROWS)
    zz = lax.rem(row // ROWS, 8)
    parity = jnp.where(second, 1 - c, c)
    real = r < jnp.where((zz == 7) & (parity == 1), VALID - 15 * CHUNK, CHUNK)
    realf = real.astype(F32)
    lane = lax.broadcasted_iota(jnp.int32, (total, 64), 1)
    ones = jnp.where(lane == 0, realf, 0.0).astype(BF)
    for h in range(3):
        vals = p_sc[v0 + h].astype(F32) * realf
        vx[h, :, 0:64] = vals.astype(BF)
        vx[h, :, 64:128] = ones

    for out_ref, base in ((oth_ref, half), (own_ref, 0)):
        for h in range(3):
            q = p_sc[q0 + h, pl.ds(base, half), :] * jnp.asarray(0.125, BF)
            s = lax.dot_general(q, p_sc[k0 + h], (((1,), (1,)), ((), ())), preferred_element_type=F32)
            m = jnp.max(s, axis=1, keepdims=True)
            p = jnp.exp(s - m).astype(BF)
            o = jnp.dot(p, vx[h], preferred_element_type=F32)
            context = o[:, 0:64] / o[:, 64:65]
            out_ref[:, 64 * h : 64 * h + 64] = context[0 : half // 2]
            out_ref[:, 192 + 64 * h : 256 + 64 * h] = context[half // 2 :]


VM = pl.BlockSpec(memory_space=pltpu.VMEM)
SM = pl.BlockSpec(memory_space=pltpu.SMEM)
TN = (((0,), (0,)), ((), ()))
NT = (((1,), (1,)), ((), ()))


def call(kernel, outs, *args, scratch=(), scalar=0, away=0, flops=0, vmem=24):
    shapes = [jax.ShapeDtypeStruct(s, d) for s, d in outs]
    moved = sum(math.prod(v.shape) * v.dtype.itemsize for v in args) + sum(math.prod(s.shape) * s.dtype.itemsize for s in shapes)
    return pl.pallas_call(
        kernel,
        out_shape=shapes,
        in_specs=[SM] * scalar + [pl.BlockSpec(memory_space=pltpu.HBM)] * away + [VM] * (len(args) - scalar - away),
        out_specs=[VM] * len(shapes),
        scratch_shapes=list(scratch),
        compiler_params=pltpu.CompilerParams(vmem_limit_bytes=vmem * 2**20),
        cost_estimate=pl.CostEstimate(flops=flops, bytes_accessed=moved, transcendentals=flops // 1000),
    )(*args)


def student_kernel(s_ref, own, nb, gain, up, down, normed, pre, hidden, br_own, br_oth, own_in):
    xl, c, g = s_ref[1], s_ref[3], s_ref[5]
    mine = c == xl

    @pl.loop(0, 8)
    def _(q):
        for b in range(2):
            for e in range(2):
                first, second = (own, nb) if b == 0 else (nb, own)
                x = jnp.where(mine, first[e, q].astype(F32), second[e, q].astype(F32))
                mean = jnp.mean(x, axis=-1, keepdims=True)
                dev = x - mean
                var = jnp.mean(dev * dev, axis=-1, keepdims=True)
                at = pl.multiple_of(256 * b + 32 * q + 16 * e, 16)
                normed[pl.ds(at, 16), :] = (dev * lax.rsqrt(var + 1e-06) * gain[...]).astype(BF)

    x = jnp.dot(normed[...], up[...], preferred_element_type=F32)
    pre[...] = x
    k0 = math.sqrt(2 / math.pi)
    hid = (x * (0.5 * (1.0 + jnp.tanh(k0 * (x + 0.044715 * (x * x * x)))))).astype(BF)
    hidden[...] = hid
    br_own[...] = lax.dot_general(hid[0:256], down[...], NT, preferred_element_type=F32)
    br_oth[...] = lax.dot_general(hid[256:512], down[...], NT, preferred_element_type=F32).astype(BF)
    own_in[...] = jnp.where(mine, own[xl, g].astype(F32), nb[xl, g].astype(F32)).astype(BF)


def join_kernel(keep, own_in, out, wide):
    total = own_in[...].astype(F32)
    for k in range(16):
        total += keep[k].astype(F32)
    row = total.astype(BF)
    out[...] = row
    for k in range(16):
        wide[k] = row


def pair_kernel(s_ref, own, other, out):
    xh = lax.rem(s_ref[5], 2)
    out[xh] = own[...]
    out[1 - xh] = other[...]


def branch_kernel(own, got, out):
    out[...] = (own[...] + got[...].astype(F32)).astype(BF)


def pack_kernel(own, got, out, a0, a1, b0, b1, mid):
    total = own[...] + got[...]
    n = total.shape[0]
    a0[0:n, :] = total[:, 0:128]
    a1[0:n, 0:64] = total[:, 128:192]
    b0[0:n, :] = total[:, 192:320]
    b1[0:n, 0:64] = total[:, 320:384]
    mid[...] = jnp.zeros_like(mid)

    @pl.loop(0, 8)
    def _(q):
        for k in range(8):
            first, second = (a0, a1) if k < 4 else (b0, b1)
            at = ROWS * (k % 4) + q
            to = 8 * q + k
            mid[to, :, 0:128] = first[pl.ds(at, 8, stride=8), :]
            mid[to, :, 128:192] = second[pl.ds(at, 8, stride=8), :][:, 0:64]
            mid[to, 0:3, 192:320] = first[pl.ds(at + 64, 3, stride=8), :]
            mid[to, 0:3, 320:384] = second[pl.ds(at + 64, 3, stride=8), :][:, 0:64]

    out[...] = mid[...].astype(BF)


def prep_kernel(s_ref, so, *refs):
    own, far = refs[:4], refs[4:8]
    w_ref, pred_ref = refs[8:]
    y, c = s_ref[0], s_ref[3]
    for d in range(4):
        base = lax.rem(y + d, 4) * 384
        for e in range(2):
            w_ref[pl.ds(pl.multiple_of(base + 192 * e + 96 * c, 96), 96), :] = own[d][e]
            w_ref[pl.ds(pl.multiple_of(base + 192 * e + 96 * (1 - c), 96), 96), :] = far[d][e]
    pred_ref[...] = lax.dot_general(so[...], w_ref[...], NT, preferred_element_type=F32)


def head_kernel(s_ref, w_hbm, sums, pred, out, w_ref, sem):
    copy = pltpu.make_async_copy(w_hbm, w_ref, sem)
    copy.start()
    g, c, z = s_ref[5], s_ref[3], s_ref[4]
    parts = []
    for k in range(8):
        total = sums[k].astype(F32)
        for m in range(1, 8):
            total += sums[8 * m + k].astype(F32)
        parts.append(jnp.concatenate([total[:, 0:192], total[:, 192:384]]))
    summed = jnp.concatenate([parts[AT[j]] for j in range(8)], axis=-1)
    row_mean = jnp.mean(summed, axis=-1, keepdims=True)
    mean_square = jnp.mean(summed * summed, axis=-1, keepdims=True)
    target = (summed - row_mean) * lax.rsqrt(mean_square - row_mean * row_mean + 1e-06)
    j = lax.broadcasted_iota(jnp.int32, (16, 1), 0)
    r = 8 * j + g
    real = (j < 11) & (r < CHUNK) & (2 * CHUNK * z + CHUNK * c + r < VALID)
    pred_grad = jnp.where(real, (pred[...] - target) * (1.0 / math.sqrt(IMAGES * VALID)), 0.0).astype(BF)
    copy.wait()
    out_grad = jnp.dot(pred_grad, w_ref[...], preferred_element_type=F32).astype(BF)
    wide = pred_grad.astype(F32)
    for k in range(8):
        for e in range(2):
            at = 192 * k + 48 * e
            out[2 * k + e, :, 0:1024] = out_grad
            cut = jnp.concatenate([wide[:, at : at + 48], wide[:, at + 96 : at + 144], jnp.zeros((16, 32), F32)], axis=-1)
            out[2 * k + e, :, 1024:1152] = cut.astype(BF)


def back_kernel(s_ref, own, far, so, so_far, hidden, pre, normed, down, out):
    c = s_ref[3]
    og = jnp.concatenate([own[:, 0:1024], far[:, 0:1024]])
    pg = jnp.concatenate([own[:, 1024:1152], far[:, 1024:1152]]).astype(F32)
    pg = jnp.where(c == 0, pg, jnp.concatenate([pg[:, 48:], pg[:, :48]], axis=-1)).astype(BF)
    head = lax.dot_general(pg, jnp.concatenate([so[...], so_far[...]]), TN, preferred_element_type=F32)[0:48]
    dn = lax.dot_general(hidden[...], og, TN, preferred_element_type=F32)
    hidden_grad = jnp.dot(og, down[...], preferred_element_type=F32)
    x = pre[...]
    k0 = math.sqrt(2 / math.pi)
    t = jnp.tanh(k0 * (x + 0.044715 * (x * x * x)))
    slope = 0.5 * (1.0 + t) + 0.5 * x * (1.0 - t * t) * (k0 * (1.0 + 3 * 0.044715 * (x * x)))
    pre_grad = (hidden_grad * slope).astype(BF)
    up = lax.dot_general(pre_grad, normed[...], TN, preferred_element_type=F32)
    a = jnp.concatenate([up, head[0:24]])
    b = jnp.concatenate([dn, head[24:48]])
    low = lax.broadcasted_iota(jnp.int32, (152, 128), 1) < 64
    for k in range(8):
        at = a[:, 128 * k : 128 * k + 128]
        bt = b[:, 128 * k : 128 * k + 128]
        out[2 * k] = jnp.where(low, at, pltpu.roll(bt, 64, 1)).astype(BF)
        out[2 * k + 1] = jnp.where(low, pltpu.roll(at, 64, 1), bt).astype(BF)


def finish_kernel(got, up, down, head):
    for e in range(2):
        total = got[e].astype(F32)
        for k in range(1, 8):
            total += got[2 * k + e].astype(F32)
        t = total.T
        up[:, 128 * e : 128 * e + 128] = t[0:64, 0:128]
        down[:, 128 * e : 128 * e + 128] = t[64:128, 0:128]
        head[:, 48 * e : 48 * e + 24] = t[0:64, 128:152]
        head[:, 48 * e + 24 : 48 * e + 48] = t[64:128, 128:152]


def halves_kernel(a, b, top, low):
    top[...] = a[...]
    low[...] = b[...]


def halves(a, b):
    shape = (a.shape[0] // 2, a.shape[1])
    first = pl.BlockSpec(shape, lambda i: (0, 0))
    return pl.pallas_call(
        halves_kernel,
        grid=(1,),
        out_shape=[jax.ShapeDtypeStruct(shape, a.dtype)] * 2,
        in_specs=[first, pl.BlockSpec(shape, lambda i: (1, 0))],
        out_specs=[first, first],
        name="halves",
    )(a, b)


def swap(x, axis):
    return lax.ppermute(x, axis, SWAP)


def turn(x, axis, n, by):
    return lax.ppermute(x, axis, [(k, (k - by) % n) for k in range(n)])


def spread(x, axis, n):
    x = jnp.broadcast_to(x[None], (n,) + x.shape)
    return lax.all_to_all(x, axis, 0, 0, tiled=True)


def after(x, *others):
    return lax.optimization_barrier((x,) + others)[0]


def inner(teacher_tokens, teacher_qkv, student_tokens, student_gain, w_up, w_down, w_head):
    y, xh, c, z, xl = (lax.axis_index(a) for a in ("y", "xh", "c", "z", "xl"))
    g = 2 * y + xh
    group = jnp.take(jnp.asarray(GROUP, jnp.int32), z)
    scalars = jnp.stack([y, xl, group % 3, c, z, g]).astype(jnp.int32)

    tt = lax.dynamic_slice_in_dim(teacher_tokens, y * 384, 384, 1).reshape(CHUNK, IMAGES, 384)
    rows = jnp.arange(ROWS)[:, None]
    reals = jnp.where((z == 7) & (xl == 1), VALID - 15 * CHUNK, CHUNK)

    def padded(v):
        v = jnp.pad(v, ((0, ROWS - CHUNK), (0, 0)))
        return jnp.where(rows < reals, v, v[79:80])

    mine = padded(jnp.where(xl == 0, tt[:, 0], tt[:, 1]))
    other = padded(jnp.where(xl == 0, tt[:, 1], tt[:, 0]))
    got = lax.ppermute(other, ("c", "xl"), [(0, 1), (3, 2)])
    piece = jnp.where(c == xl, mine, got)
    xa0 = spread(piece, "z", 8).reshape(8 * ROWS, 384)
    xa1 = turn(xa0, "y", 4, 1)
    xa3 = turn(xa0, "y", 4, 3)
    top, low = halves(xa1, xa3)
    xa2 = turn(top, "y", 4, 1)
    xa2l = turn(low, "y", 4, 3)
    xa = (xa0, xa1, xa2, xa2l, xa3)
    xb = tuple(swap(v, "c") for v in xa)

    wt = teacher_qkv[0].T
    main = jnp.where(xl == 0, wt[:192], wt[96:])
    part = jnp.where(xl == 0, wt[192:], wt[:96])
    to_main = [(2 * k + e, 2 * AT[(3 * k + 2 * e) % 8] + e) for k in range(8) for e in range(2)]
    to_part = [(2 * k + e, 2 * AT[(3 * k + 1) % 8] + e) for k in range(8) for e in range(2)]
    m_own = lax.ppermute(main, DP, to_main)
    h_own = lax.ppermute(part, DP, to_part)
    m_oth = swap(m_own, "xl")
    h_oth = swap(h_own, "xl")

    def arranged(v):
        v = jnp.pad(v, ((0, (128 - CHUNK) * IMAGES), (0, 0))).reshape(16, 8, IMAGES, -1)
        return v.transpose(2, 1, 0, 3)

    st_own = arranged(student_tokens)
    st_nb = swap(st_own, "xl")
    up = lax.dynamic_slice_in_dim(w_up, xl * 128, 128, 1)
    down = lax.dynamic_slice_in_dim(w_down, xl * 128, 128, 1)
    normed, pre, hidden, br_own, br_oth, own_in = call(
        student_kernel,
        [((512, 1024), BF), ((512, 128), F32), ((512, 128), BF), ((256, 1024), F32), ((256, 1024), BF), ((16, 1024), BF)],
        scalars, st_own, st_nb, student_gain[None], up, down, scalar=1, flops=300_000_000,
    )
    (keep,) = call(branch_kernel, [((256, 1024), BF)], br_own, swap(br_oth, "c"))
    keep = keep.reshape(16, 16, -1)
    keep = lax.all_to_all(keep, ("y", "xh", "xl"), 0, 0, tiled=True)
    student_out, wide = call(join_kernel, [((16, 1024), BF), ((16, 16, 1024), BF)], keep, own_in)
    so_own = lax.all_to_all(wide, ("y", "xh", "xl"), 0, 0, tiled=True).reshape(256, -1)
    so_far = swap(so_own, "c")

    wh = w_head.T
    wh2 = swap(wh, "xh")
    (pair,) = call(pair_kernel, [((2, 96, 1024), BF)], scalars, wh, wh2, scalar=1)
    w_own = [pair] + [turn(pair, "y", 4, k) for k in (1, 2, 3)]
    w_far = [swap(v, "c") for v in w_own]

    t_scalars = after(scalars, student_out)
    half = 8 * ROWS
    total = 2 * half
    own, oth = call(
        teacher_kernel, [((half // 2, 384), F32)] * 2, t_scalars, *xa, *xb, m_own, m_oth, h_own, h_oth,
        scratch=[
            pltpu.VMEM((total, 1536), BF),
            pltpu.VMEM((576, 1536), BF),
            pltpu.VMEM((9, total, 64), BF),
            pltpu.VMEM((3, total, 128), BF),
        ],
        scalar=1, flops=6_000_000_000, vmem=34,
    )
    got = swap(oth, "c")
    (both,) = call(
        pack_kernel, [((64, 8, 384), BF)], own, got,
        scratch=[pltpu.VMEM((half // 2 + 48, 128), F32)] * 4 + [pltpu.VMEM((64, 8, 384), F32)],
    )
    both = after(both, so_own)
    sums = lax.all_to_all(both, ("y", "xh", "z"), 0, 0, tiled=True)

    w_all, pred = call(
        prep_kernel, [((1536, 1024), BF), ((16, 1536), F32)], scalars, student_out, *w_own, *w_far, scalar=1
    )
    (load,) = call(
        head_kernel, [((16, 16, 1152), BF)], scalars, w_all, sums, pred,
        scratch=[pltpu.VMEM((1536, 1024), BF), pltpu.SemaphoreType.DMA], scalar=1, away=1, vmem=58,
    )
    load = lax.all_to_all(load, ("y", "xh", "xl"), 0, 0, tiled=True).reshape(256, 1152)
    far = swap(load, "c")

    (grads,) = call(
        back_kernel, [((16, 152, 128), BF)], scalars, load, far, so_own, so_far, hidden, pre, normed, down, scalar=1
    )
    grads = lax.all_to_all(grads, DP, 0, 0, tiled=True)
    return tuple(call(finish_kernel, [((64, 256), F32), ((64, 256), F32), ((64, 96), F32)], grads))


def solution(mesh):
    fine = Mesh(mesh.devices.reshape(4, 2, 2, 8, 2), ("y", "xh", "c", "z", "xl"))
    in_specs = (
        P(DP, None),
        P(MEM, None, DP),
        P(DP, None),
        P(),
        P(None, MEM),
        P(None, MEM),
        P(None, MEM),
    )
    out_specs = (P(DP, MEM), P(DP, MEM), P(DP, MEM))
    return jax.shard_map(inner, mesh=fine, in_specs=in_specs, out_specs=out_specs, check_vma=False)
```
